512 devices in a mesh: chan: 64 (over x, y, core), src: 8 (over z).
Axes of the slice: x: 4, y: 8, z: 8, core: 2. Of those that a mesh axis runs over, the one named last changes fastest.
Arguments:
- strain: bfloat16 [4096, 65536], P('src', 'chan'), may hold values from -6 to 6
- seg_start: int32 [3], replicated, may hold values from 0 to 8704
- src_chan: int32 [256], replicated, may hold values from 0 to 4095
Outputs:
- correlation: bfloat16 [256, 8, 512, 512], P('src', None, 'chan')
The draws below stay inside these ranges and needn't reach their ends.
All inputs are finite; a program needn't handle non-finite values.
Results may differ from the reference program's by a relative error of at most 0.0083.
Values may be sent and summed in bfloat16 or wider, within the bound.
A program may use at most 64 MiB of HBM per device.

```python
import math
import jax
import jax.numpy as jnp
import numpy as np
from jax import lax

NT = 65536
DEC = 4
SEG = 7680
NSEG = 3
BIN_LOW = 61
NBIN = 384
NLAG = 512
NSRC = 256
NTD = 16384
NCH = 4096
N_SRC = 8


def touch_ends(array, key, smallest, largest):
    dims = array.shape
    spot = [jax.random.randint(jax.random.fold_in(key, axis), (), 0, dims[axis]) for axis in range(len(dims))]
    array = array.at[tuple(spot)].set(smallest)
    longest = dims.index(max(dims))
    spot[longest] = (spot[longest] + 1) % dims[longest]
    return array.at[tuple(spot)].set(largest)


def shard_levels(own_key, extent, shards, least, largest):
    factor_of, own = 1.0, jax.random.fold_in(own_key, 6)
    for position, shards_of in shards:
        draws = jnp.exp(jax.random.uniform(jax.random.fold_in(own, position), (shards_of,), jnp.float32, least / len(shards), largest / len(shards)))
        factor_of = factor_of * jnp.repeat(draws, extent[position] // shards_of).reshape([-1 if axis == position else 1 for axis in range(len(extent))])
    return factor_of


def bell_draw(own_key, dims, deviation, limit, cuts=(), kind=jnp.bfloat16):
    drawn = jax.random.normal(own_key, dims, jnp.float32) * deviation
    if len(cuts) > 0:
        drawn = shard_levels(own_key, dims, cuts, -0.22, 0.18) * drawn
    return jnp.clip(drawn, min=-limit, max=limit).astype(kind)


def setup_inputs(seed: int = 0) -> dict:
    key_list = jax.random.split(jax.random.key(seed), 4)
    strain = bell_draw(key_list[0], (NCH, NT), 1.0, 6.0, ((0, 8), (1, 64)))
    seg_start = jax.random.randint(key_list[1], (NSEG,), 0, NTD - SEG + 1).astype(jnp.int32)
    src_chan = touch_ends(jax.random.randint(key_list[2], (NSRC,), 0, NCH), jax.random.fold_in(key_list[2], 1), 0, NCH - 1).astype(jnp.int32)
    return dict(strain=strain, seg_start=seg_start, src_chan=src_chan)


def decimation_tables():
    length = 4 * DEC
    offsets = np.arange(length)
    centred = (offsets - (length - 1) / 2.0) / DEC
    coeffs = np.sin(np.pi * centred) / (np.pi * centred) * (0.54 - 0.46 * np.cos(2.0 * np.pi * (offsets + 0.5) / length))
    coeffs = coeffs / coeffs.sum()
    sample_pos = np.arange(128)[:, None]
    output_pos = np.arange(128 // DEC)[None, :]
    tables = []
    for carried in (0, 128):
        tap_pos = sample_pos + carried - DEC * output_pos
        inside = (tap_pos >= 0) & (tap_pos < length)
        values = np.where(inside, coeffs[np.clip(tap_pos, 0, length - 1)], 0.0)
        tables.append(jnp.asarray(values, jnp.float32).astype(jnp.bfloat16))
    return (tables[0], tables[1])

def decimate(series, following, first_tab, second_tab):
    row_count, length = series.shape
    blocks = series.reshape(row_count, length // 128, 128)
    shifted = jnp.concatenate([blocks[:, 1:], following[:, None, :]], axis=1)
    summed = jnp.dot(blocks.reshape(-1, 128), first_tab, preferred_element_type=jnp.float32)
    summed = summed + jnp.dot(shifted.reshape(-1, 128), second_tab, preferred_element_type=jnp.float32)
    return summed.astype(jnp.bfloat16).reshape(row_count, length // DEC)

def whiten(spectrum):
    real_part = spectrum[..., :NBIN]
    imag_part = spectrum[..., NBIN:]
    energy = real_part * real_part + imag_part * imag_part
    offsets = np.arange(NBIN)
    band_mask = jnp.asarray((np.abs(offsets[:, None] - offsets[None, :]) <= 32).astype(np.float32))
    smooth = jnp.matmul(energy, band_mask, precision=lax.Precision.HIGHEST) / 65.0
    inverse = lax.rsqrt(smooth + 1e-05)
    return jnp.concatenate([real_part * inverse, imag_part * inverse], axis=-1).astype(jnp.bfloat16)

def lag_table():
    bin_ids = BIN_LOW + np.arange(NBIN)
    delays = np.arange(NLAG) - NLAG // 2
    angles = 2.0 * np.pi * np.mod(np.outer(bin_ids, delays), SEG) / SEG
    basis = np.concatenate([np.cos(angles), -np.sin(angles)], axis=0) / np.sqrt(NBIN)
    return jnp.asarray(basis, jnp.float32).astype(jnp.bfloat16)

def reference(strain, seg_start, src_chan):
    channels, samples = strain.shape
    block_rows = math.gcd(channels, 64)
    first_tab, second_tab = decimation_tables()

    def spectra_of(strain_block):
        padding = jnp.zeros((block_rows, 128), jnp.bfloat16)
        decimated = decimate(strain_block, padding, first_tab, second_tab)
        pieces = [lax.dynamic_slice_in_dim(decimated, seg_start[number], SEG, 1) for number in range(NSEG)]
        segments = jnp.stack(pieces, axis=1).astype(jnp.float32)
        transform = jnp.fft.rfft(segments, axis=-1)[..., BIN_LOW:BIN_LOW + NBIN] / math.sqrt(SEG)
        spectrum = jnp.concatenate([jnp.real(transform), jnp.imag(transform)], axis=-1)
        return whiten(spectrum)
    spectra = lax.map(spectra_of, strain.reshape(channels // block_rows, block_rows, samples))
    receivers = spectra.reshape(channels, NSEG, 2 * NBIN).astype(jnp.float32)
    sources = receivers[src_chan]
    basis = lag_table()
    recv_re = receivers[..., :NBIN]
    recv_im = receivers[..., NBIN:]
    highest = lax.Precision.HIGHEST

    def per_group(source_block):
        source_re = source_block[..., :NBIN]
        source_im = source_block[..., NBIN:]
        cross_re = jnp.einsum('ksf,rsf->krf', source_re, recv_re, precision=highest)
        cross_re = (cross_re + jnp.einsum('ksf,rsf->krf', source_im, recv_im, precision=highest)) / NSEG
        cross_im = jnp.einsum('ksf,rsf->krf', source_re, recv_im, precision=highest)
        cross_im = (cross_im - jnp.einsum('ksf,rsf->krf', source_im, recv_re, precision=highest)) / NSEG
        merged = jnp.concatenate([cross_re, cross_im], axis=-1).astype(jnp.bfloat16)
        lagged = jnp.dot(merged.reshape(-1, 2 * NBIN), basis, preferred_element_type=jnp.float32)
        return lagged.astype(jnp.bfloat16).reshape(source_block.shape[0], channels, NLAG)
    result = lax.map(per_group, sources.reshape(NSRC // 8, 8, NSEG, 2 * NBIN))
    return result.reshape(NSRC, N_SRC, channels // N_SRC, NLAG)
```

```python
import math

import jax
import jax.numpy as jnp
import numpy as np
from jax import lax
from jax.experimental import pallas as pl
from jax.experimental.pallas import tpu as pltpu
from jax.sharding import PartitionSpec as P

DEC = 4
SEG = 7680
NSEG = 3
BIN_LOW = 61
NBIN = 384
NLAG = 512
TAPS = 16
WIN = 31


def taps():
    offsets = np.arange(TAPS)
    centred = (offsets - (TAPS - 1) / 2.0) / DEC
    coeffs = (
        np.sin(np.pi * centred)
        / (np.pi * centred)
        * (0.54 - 0.46 * np.cos(2.0 * np.pi * (offsets + 0.5) / TAPS))
    )
    return coeffs / coeffs.sum()


def band_table(samples, outputs, shift):
    coeffs = taps()
    tap = np.arange(samples)[:, None] + shift - DEC * np.arange(outputs)[None, :]
    inside = (tap >= 0) & (tap < TAPS)
    values = np.where(inside, coeffs[np.clip(tap, 0, TAPS - 1)], 0.0)
    return jnp.asarray(values, jnp.float32).astype(jnp.bfloat16)


def lag_table():
    bin_ids = BIN_LOW + np.arange(NBIN)
    delays = np.arange(NLAG) - NLAG // 2
    angles = 2.0 * np.pi * np.mod(np.outer(bin_ids, delays), SEG) / SEG
    basis = np.concatenate([np.cos(angles), -np.sin(angles)], axis=0) / np.sqrt(NBIN)
    return jnp.asarray(basis, jnp.float32).astype(jnp.bfloat16)


def inner_tables(width):
    bin_ids = BIN_LOW + np.arange(NBIN)
    inner = 2.0 * np.pi * np.mod(np.outer(np.arange(width), bin_ids), SEG) / SEG
    table = jnp.asarray(np.concatenate([np.cos(inner), -np.sin(inner)], axis=1), jnp.float32)
    high = table.astype(jnp.bfloat16)
    low = (table - high.astype(jnp.float32)).astype(jnp.bfloat16)
    return high, low


def outer_tables(width, count):
    bin_ids = BIN_LOW + np.arange(NBIN)
    outer = 2.0 * np.pi * np.mod(np.outer(width * np.arange(count), bin_ids), SEG) / SEG
    return jnp.asarray(np.cos(outer), jnp.float32), jnp.asarray(np.sin(outer), jnp.float32)


def whiten(real_part, imag_part):
    energy = real_part * real_part + imag_part * imag_part
    offsets = np.arange(NBIN)
    band_mask = jnp.asarray((np.abs(offsets[:, None] - offsets[None, :]) <= 32).astype(np.float32))
    smooth = jnp.matmul(energy, band_mask, precision=lax.Precision.HIGHEST) / 65.0
    inverse = lax.rsqrt(smooth + 1e-05)
    return jnp.concatenate([real_part * inverse, imag_part * inverse], axis=-1).astype(jnp.bfloat16)


def correlate_kernel(per_step, src_ref, recv_ref, basis_ref, out_ref, merged):
    rows = recv_ref.shape[1]
    chunk = 16
    for number in range(per_step):
        for low in range(0, rows, chunk):
            total_re = jnp.zeros((chunk, NBIN), jnp.float32)
            total_im = jnp.zeros((chunk, NBIN), jnp.float32)
            for seg in range(NSEG):
                a = src_ref[number, seg : seg + 1, :]
                a_re = a[:, :NBIN]
                a_im = a[:, NBIN:]
                b = recv_ref[seg, low : low + chunk, :].astype(jnp.float32)
                b_re = b[:, :NBIN]
                b_im = b[:, NBIN:]
                total_re += a_re * b_re + a_im * b_im
                total_im += a_re * b_im - a_im * b_re
            spot = number * rows + low
            merged[spot : spot + chunk, :NBIN] = (total_re * (1.0 / NSEG)).astype(jnp.bfloat16)
            merged[spot : spot + chunk, NBIN:] = (total_im * (1.0 / NSEG)).astype(jnp.bfloat16)
    lagged = jnp.dot(merged[...], basis_ref[...], preferred_element_type=jnp.float32)
    out_ref[...] = lagged.astype(jnp.bfloat16)


def correlate(sources, receivers, per_step=4):
    count = sources.shape[0]
    rows = receivers.shape[1]
    return pl.pallas_call(
        lambda *refs: correlate_kernel(per_step, *refs),
        grid=(count // per_step,),
        in_specs=[
            pl.BlockSpec((per_step, NSEG, 2 * NBIN), lambda i: (i, 0, 0)),
            pl.BlockSpec((NSEG, rows, 2 * NBIN), lambda i: (0, 0, 0)),
            pl.BlockSpec((2 * NBIN, NLAG), lambda i: (0, 0)),
        ],
        out_specs=pl.BlockSpec((per_step * rows, NLAG), lambda i: (i, 0)),
        out_shape=jax.ShapeDtypeStruct((count * rows, NLAG), jnp.bfloat16),
        scratch_shapes=[pltpu.VMEM((per_step * rows, 2 * NBIN), jnp.bfloat16)],
        name="correlate",
    )(sources, receivers, lag_table())


def on_device(strain, seg_start, src_chan):
    chan_count = lax.axis_size("chan")
    group_count = lax.axis_size("src")
    local_rows, local_samples = strain.shape
    per_device = local_rows // chan_count
    width = local_samples // DEC
    carried = TAPS - DEC
    carried_out = carried // DEC
    partial_back = jnp.dot(
        strain[:, :carried],
        band_table(carried, carried_out, carried),
        preferred_element_type=jnp.float32,
    )
    partial_back = lax.ppermute(
        partial_back.T.astype(jnp.bfloat16),
        "chan",
        [(number, number - 1) for number in range(1, chan_count)],
    )
    decimated = jnp.dot(
        strain, band_table(local_samples, width, 0), preferred_element_type=jnp.float32
    )
    decimated = decimated + jnp.pad(
        partial_back.T.astype(jnp.float32), ((0, 0), (width - carried_out, 0))
    )
    decimated = decimated.astype(jnp.bfloat16)
    plane_channels = lax.axis_index("src") * local_rows + lax.iota(jnp.int32, local_rows)
    selector = (src_chan[:, None] == plane_channels[None, :]).astype(jnp.bfloat16)
    picked = jnp.dot(selector, decimated, preferred_element_type=jnp.float32).astype(jnp.bfloat16)
    picked = picked.reshape(group_count, -1, width)
    pieces = lax.all_to_all(picked, "src", split_axis=0, concat_axis=0, tiled=True)
    own = jnp.sum(pieces.astype(jnp.float32), axis=0).astype(jnp.bfloat16)
    own_count = own.shape[0]
    share = chan_count // own_count
    outgoing = jnp.concatenate(
        [
            decimated.reshape(chan_count, per_device, width),
            jnp.repeat(own, share, axis=0)[:, None, :],
        ],
        axis=1,
    )
    series = lax.all_to_all(outgoing, "chan", split_axis=0, concat_axis=0, tiled=True)
    series = jnp.pad(series, ((0, 1), (0, 0), (0, 0)))
    aligned = seg_start // width
    offset = seg_start - aligned * width
    position = (width * np.arange(WIN)[:, None] + np.arange(width)[None, :])[:, None, :]
    pieces = []
    for number in range(NSEG):
        window = lax.dynamic_slice_in_dim(series, aligned[number], WIN, 0)
        inside = (position >= offset[number]) & (position < offset[number] + SEG)
        pieces.append(jnp.where(inside, window, jnp.zeros((), jnp.bfloat16)))
    flat = jnp.stack(pieces, axis=0).reshape(-1, width)
    high, low = inner_tables(width)
    part = jnp.dot(flat, high, preferred_element_type=jnp.float32)
    part = part + jnp.dot(flat, low, preferred_element_type=jnp.float32)
    part = part.reshape(NSEG, WIN, per_device + 1, 2 * NBIN)
    phase_cos, phase_sin = outer_tables(width, WIN)
    phase_cos = phase_cos[:, None, :]
    phase_sin = phase_sin[:, None, :]
    part_re = part[..., :NBIN]
    part_im = part[..., NBIN:]
    scale = 1.0 / math.sqrt(SEG)
    total_re = jnp.sum(part_re * phase_cos + part_im * phase_sin, axis=1) * scale
    total_im = jnp.sum(part_im * phase_cos - part_re * phase_sin, axis=1) * scale
    spectra = whiten(total_re, total_im)
    own_recv = spectra[:, :per_device]
    own_src = spectra[:, per_device]
    receivers = lax.all_to_all(
        jnp.broadcast_to(own_recv[None], (group_count,) + own_recv.shape),
        "src",
        split_axis=0,
        concat_axis=0,
        tiled=True,
    )
    receivers = receivers.transpose(1, 0, 2, 3).reshape(NSEG, -1, 2 * NBIN)
    sources = lax.all_to_all(
        jnp.broadcast_to(own_src.reshape(1, -1), (chan_count, own_src.size)),
        "chan",
        split_axis=0,
        concat_axis=0,
        tiled=True,
    )
    sources = sources.reshape(own_count, share, NSEG, 2 * NBIN)[:, 0].astype(jnp.float32)
    lagged = correlate(sources, receivers)
    return lagged.reshape(own_count, group_count, per_device, NLAG)


def solution(mesh):
    return jax.shard_map(
        on_device,
        mesh=mesh,
        in_specs=(P("src", "chan"), P(), P()),
        out_specs=P("src", None, "chan", None),
        check_vma=False,
    )
```

```python
import functools
import math

import jax
import jax.numpy as jnp
import numpy as np
from jax import lax
from jax.experimental import pallas as pl
from jax.experimental.pallas import tpu as pltpu
from jax.sharding import PartitionSpec as P

DEC = 4
SEG = 7680
NSEG = 3
BIN_LOW = 61
NBIN = 384
NLAG = 512
TAPS = 16
WIN = 31
WIDTH = 256

MESH = pl.DeviceIdType.MESH


def taps():
    offsets = np.arange(TAPS)
    centred = (offsets - (TAPS - 1) / 2.0) / DEC
    coeffs = (
        np.sin(np.pi * centred)
        / (np.pi * centred)
        * (0.54 - 0.46 * np.cos(2.0 * np.pi * (offsets + 0.5) / TAPS))
    )
    return coeffs / coeffs.sum()


def band_table(samples, outputs, shift):
    coeffs = taps()
    tap = np.arange(samples)[:, None] + shift - DEC * np.arange(outputs)[None, :]
    inside = (tap >= 0) & (tap < TAPS)
    values = np.where(inside, coeffs[np.clip(tap, 0, TAPS - 1)], 0.0)
    return jnp.asarray(values, jnp.float32).astype(jnp.bfloat16)


def lag_table():
    bin_ids = BIN_LOW + np.arange(NBIN)
    delays = np.arange(NLAG) - NLAG // 2
    angles = 2.0 * np.pi * np.mod(np.outer(bin_ids, delays), SEG) / SEG
    basis = np.concatenate([np.cos(angles), -np.sin(angles)], axis=0) / np.sqrt(NBIN)
    return jnp.asarray(basis, jnp.float32).astype(jnp.bfloat16)


def inner_tables(width):
    bin_ids = BIN_LOW + np.arange(NBIN)
    inner = 2.0 * np.pi * np.mod(np.outer(np.arange(width), bin_ids), SEG) / SEG
    table = jnp.asarray(np.concatenate([np.cos(inner), -np.sin(inner)], axis=1), jnp.float32)
    high = table.astype(jnp.bfloat16)
    low = (table - high.astype(jnp.float32)).astype(jnp.bfloat16)
    return high, low


def outer_tables(width, count):
    bin_ids = BIN_LOW + np.arange(NBIN)
    outer = 2.0 * np.pi * np.mod(np.outer(width * np.arange(count), bin_ids), SEG) / SEG
    return jnp.asarray(np.cos(outer), jnp.float32), jnp.asarray(np.sin(outer), jnp.float32)


def smooth_mask():
    offsets = np.arange(NBIN)
    near = np.abs(offsets[:, None] - offsets[None, :]) <= 32
    return jnp.asarray(near.astype(np.float32)).astype(jnp.bfloat16)


def halo_tables():
    carried = TAPS - DEC
    outs = carried // DEC
    coeffs = taps()
    tap = np.arange(128)[None, :] + carried - DEC * np.arange(16)[:, None]
    inside = (tap >= 0) & (tap < TAPS) & (np.arange(16)[:, None] < outs)
    back = np.where(inside, coeffs[np.clip(tap, 0, TAPS - 1)], 0.0)
    place = np.zeros((16, 128))
    place[np.arange(outs), 128 - outs + np.arange(outs)] = 1.0
    return (
        jnp.asarray(back, jnp.float32).astype(jnp.bfloat16),
        jnp.asarray(place, jnp.float32).astype(jnp.bfloat16),
    )


def spectra_of(series, seg_ref, high_ref, low_ref, cos_ref, sin_ref, mask_ref, windows, result):
    lane = lax.broadcasted_iota(jnp.int32, (8, WIDTH), 1)
    for number in range(NSEG):
        start = seg_ref[number]
        first = lax.shift_right_logical(start, 8)
        offset = lax.bitwise_and(start, 255)
        window = series[pl.ds(first, WIN)].astype(jnp.float32)
        base = number * WIN * 8
        windows[base : base + 8, :] = jnp.where(lane >= offset, window[0], 0.0)
        middle = window[1 : WIN - 1].reshape((WIN - 2) * 8, WIDTH)
        windows[base + 8 : base + (WIN - 1) * 8, :] = middle
        windows[base + (WIN - 1) * 8 : base + WIN * 8, :] = jnp.where(
            lane < offset, window[WIN - 1], 0.0
        )
    flat = windows[...].astype(jnp.bfloat16)
    part = jnp.dot(flat, high_ref[...], preferred_element_type=jnp.float32)
    result[...] = part + jnp.dot(flat, low_ref[...], preferred_element_type=jnp.float32)
    scale = 1.0 / math.sqrt(SEG)
    reals, imags = [], []
    for number in range(NSEG):
        total_re = jnp.zeros((8, NBIN), jnp.float32)
        total_im = jnp.zeros((8, NBIN), jnp.float32)
        for block in range(WIN):
            base = (number * WIN + block) * 8
            part_re = result[base : base + 8, :NBIN]
            part_im = result[base : base + 8, NBIN:]
            phase_cos = cos_ref[block : block + 1, :]
            phase_sin = sin_ref[block : block + 1, :]
            total_re += part_re * phase_cos + part_im * phase_sin
            total_im += part_im * phase_cos - part_re * phase_sin
        reals.append(total_re * scale)
        imags.append(total_im * scale)
    real_part = jnp.concatenate(reals, axis=0)
    imag_part = jnp.concatenate(imags, axis=0)
    energy = real_part * real_part + imag_part * imag_part
    smooth = jnp.zeros((NSEG * 8, NBIN), jnp.float32)
    for _ in range(3):
        piece = energy.astype(jnp.bfloat16)
        smooth += jnp.dot(piece, mask_ref[...], preferred_element_type=jnp.float32)
        energy = energy - piece.astype(jnp.float32)
    inverse = lax.rsqrt(smooth / 65.0 + 1e-05)
    white = jnp.concatenate([real_part * inverse, imag_part * inverse], axis=1)
    return white.reshape(NSEG, 8, 2 * NBIN).astype(jnp.bfloat16)


def front_kernel(
    chan_count,
    group_count,
    seg_ref,
    src_ref,
    strain,
    band,
    back,
    place,
    high,
    low,
    cos_ref,
    sin_ref,
    mask,
    recv_out,
    src_out,
    dec,
    series,
    halo_send,
    halo_recv,
    picks,
    picked,
    tiles,
    src_series,
    white,
    gathered,
    src_white,
    src_gathered,
    windows,
    result,
    send,
    recv,
    send_src_sem,
):
    me = lax.axis_index("chan")
    plane = lax.axis_index("src")
    rows = strain.shape[0]

    barrier = pltpu.get_barrier_semaphore()

    def greet_chan(step, carry):
        peer = lax.rem(me + step, chan_count)
        pl.semaphore_signal(barrier, inc=1, device_id={"chan": peer}, device_id_type=MESH)
        return carry

    def greet_src(step, carry):
        peer = lax.rem(plane + step, group_count)
        pl.semaphore_signal(barrier, inc=1, device_id={"src": peer}, device_id_type=MESH)
        return carry

    lax.fori_loop(1, chan_count, greet_chan, 0)
    lax.fori_loop(1, group_count, greet_src, 0)

    halo_send[...] = lax.dot_general(
        back[...],
        strain[:, :128],
        (((1,), (1,)), ((), ())),
        preferred_element_type=jnp.float32,
    ).astype(jnp.bfloat16)
    decimated = jnp.dot(strain[...], band[...], preferred_element_type=jnp.float32)
    series[chan_count] = jnp.zeros((8, WIDTH), jnp.bfloat16)
    channel = lax.broadcasted_iota(jnp.int32, (src_ref.shape[0], rows), 1) + plane * rows
    selector = (src_ref[...] == channel).astype(jnp.float32).astype(jnp.bfloat16)

    pl.semaphore_wait(barrier, chan_count - 1 + group_count - 1)

    before = lax.rem(me + chan_count - 1, chan_count)
    halo = pltpu.make_async_remote_copy(
        halo_send, halo_recv, send.at[0], recv.at[0], {"chan": before}, MESH
    )
    halo.start()
    halo.wait()
    last = jnp.where(me == chan_count - 1, 0.0, 1.0)
    tail = halo_recv[...].astype(jnp.float32) * last
    tail = jnp.dot(
        tail.T.astype(jnp.bfloat16), place[...], preferred_element_type=jnp.float32
    )
    decimated = jnp.concatenate([decimated[:, :128], decimated[:, 128:] + tail], axis=1)
    dec[...] = decimated.reshape(chan_count, 8, WIDTH).astype(jnp.bfloat16)

    def send_chan(step, carry):
        peer = lax.rem(me + step, chan_count)
        pltpu.make_async_remote_copy(
            dec.at[peer], series.at[me], send.at[1], recv.at[1], {"chan": peer}, MESH
        ).start()
        return carry

    lax.fori_loop(1, chan_count, send_chan, 0)
    series[me] = dec[me]

    chosen = jnp.dot(selector, decimated.astype(jnp.bfloat16), preferred_element_type=jnp.float32)
    picks[...] = chosen.reshape(group_count, -1, WIDTH).astype(jnp.bfloat16)

    def send_picks(step, carry):
        peer = lax.rem(plane + step, group_count)
        pltpu.make_async_remote_copy(
            picks.at[peer], picked.at[plane], send.at[2], recv.at[2], {"src": peer}, MESH
        ).start()
        return carry

    lax.fori_loop(1, group_count, send_picks, 0)
    picked[plane] = picks[plane]
    others = pl.ds(0, group_count - 1)
    pltpu.make_async_remote_copy(
        picks.at[others], picked.at[others], send.at[2], recv.at[2], {"src": plane}, MESH
    ).wait()
    own = picked[0].astype(jnp.float32)
    for number in range(1, group_count):
        own += picked[number].astype(jnp.float32)
    tiles[...] = own.reshape(-1, 8, WIDTH).astype(jnp.bfloat16)

    is_owner = lax.rem(me, 4) == 0
    owner_count = chan_count // 4

    def send_tiles(step, carry):
        peer = lax.rem(me + 4 * step - lax.rem(me, 4) + 4, chan_count)

        @pl.when(peer != me)
        def _():
            pltpu.make_async_remote_copy(
                tiles.at[lax.div(peer, 16)],
                src_series.at[me],
                send.at[3],
                recv.at[3],
                {"chan": peer},
                MESH,
            ).start()

        return carry

    lax.fori_loop(0, owner_count, send_tiles, 0)

    everyone = pl.ds(0, chan_count - 1)
    pltpu.make_async_remote_copy(
        dec.at[everyone], series.at[everyone], send.at[1], recv.at[1], {"chan": me}, MESH
    ).wait()
    white[...] = spectra_of(series, seg_ref, high, low, cos_ref, sin_ref, mask, windows, result)

    def send_white(step, carry):
        peer = lax.rem(plane + step, group_count)
        pltpu.make_async_remote_copy(
            white, gathered.at[plane], send.at[4], recv.at[4], {"src": peer}, MESH
        ).start()
        return carry

    lax.fori_loop(1, group_count, send_white, 0)
    gathered[plane] = white[...]

    column = lax.div(me, 16)
    region = lax.div(lax.rem(me, 16), 4)

    @pl.when(is_owner)
    def _():
        src_series[me] = tiles[column]
        src_series[chan_count] = jnp.zeros((8, WIDTH), jnp.bfloat16)
        pltpu.make_async_remote_copy(
            src_series.at[everyone],
            src_series.at[everyone],
            send.at[3],
            recv.at[3],
            {"chan": me},
            MESH,
        ).wait_recv()
        src_white[...] = spectra_of(
            src_series, seg_ref, high, low, cos_ref, sin_ref, mask, windows, result
        )

        def send_src(step, carry):
            peer = 16 * lax.div(step, 4) + 4 * region + lax.rem(step, 4)

            @pl.when(peer != me)
            def _():
                pltpu.make_async_remote_copy(
                    src_white,
                    src_gathered.at[column],
                    send_src_sem.at[step],
                    recv.at[5],
                    {"chan": peer},
                    MESH,
                ).start()

            return carry

        lax.fori_loop(0, 16, send_src, 0)
        src_gathered[column] = src_white[...]

    pltpu.make_async_remote_copy(
        gathered.at[others], gathered.at[others], send.at[4], recv.at[4], {"src": plane}, MESH
    ).wait()
    recv_out[...] = gathered[...]

    def wait_src(count):
        part = src_gathered.at[pl.ds(0, count)]
        return pltpu.make_async_remote_copy(
            part, part, send.at[4], recv.at[5], {"chan": me}, MESH
        )

    @pl.when(is_owner)
    def _():
        wait_src(3).wait_recv()

        def sent_src(step, carry):
            peer = 16 * lax.div(step, 4) + 4 * region + lax.rem(step, 4)

            @pl.when(peer != me)
            def _():
                pltpu.make_async_remote_copy(
                    src_white,
                    src_gathered.at[column],
                    send_src_sem.at[step],
                    recv.at[5],
                    {"chan": peer},
                    MESH,
                ).wait_send()

            return carry

        lax.fori_loop(0, 16, sent_src, 0)
        sent = tiles_wait(src_series, chan_count, owner_count - 1)
        pltpu.make_async_remote_copy(sent, sent, send.at[3], recv.at[3], {"chan": me}, MESH).wait_send()

    @pl.when(jnp.logical_not(is_owner))
    def _():
        wait_src(4).wait_recv()
        sent = tiles_wait(src_series, chan_count, owner_count)
        pltpu.make_async_remote_copy(sent, sent, send.at[3], recv.at[3], {"chan": me}, MESH).wait_send()

    src_out[...] = src_gathered[...]


def tiles_wait(ref, chan_count, count):
    return ref.at[pl.ds(0, count)]


def front(strain, seg_start, src_chan, chan_count, group_count):
    count = src_chan.shape[0]
    share = count // group_count
    back, place = halo_tables()
    high, low = inner_tables(WIDTH)
    phase_cos, phase_sin = outer_tables(WIDTH, WIN)
    vmem = pl.BlockSpec(memory_space=pltpu.VMEM)
    half = jnp.bfloat16
    return pl.pallas_call(
        functools.partial(front_kernel, chan_count, group_count),
        out_shape=(
            jax.ShapeDtypeStruct((group_count, NSEG, 8, 2 * NBIN), half),
            jax.ShapeDtypeStruct((share // 8, NSEG, 8, 2 * NBIN), half),
        ),
        in_specs=[pl.BlockSpec(memory_space=pltpu.SMEM)] + [vmem] * 10,
        out_specs=(vmem, vmem),
        scratch_shapes=[
            pltpu.VMEM((chan_count, 8, WIDTH), half),
            pltpu.VMEM((chan_count + 1, 8, WIDTH), half),
            pltpu.VMEM((16, strain.shape[0]), half),
            pltpu.VMEM((16, strain.shape[0]), half),
            pltpu.VMEM((group_count, share, WIDTH), half),
            pltpu.VMEM((group_count, share, WIDTH), half),
            pltpu.VMEM((share // 8, 8, WIDTH), half),
            pltpu.VMEM((chan_count + 1, 8, WIDTH), half),
            pltpu.VMEM((NSEG, 8, 2 * NBIN), half),
            pltpu.VMEM((group_count, NSEG, 8, 2 * NBIN), half),
            pltpu.VMEM((NSEG, 8, 2 * NBIN), half),
            pltpu.VMEM((share // 8, NSEG, 8, 2 * NBIN), half),
            pltpu.VMEM((NSEG * WIN * 8, WIDTH), jnp.float32),
            pltpu.VMEM((NSEG * WIN * 8, 2 * NBIN), jnp.float32),
            pltpu.SemaphoreType.DMA((5,)),
            pltpu.SemaphoreType.DMA((6,)),
            pltpu.SemaphoreType.DMA((16,)),
        ],
        compiler_params=pltpu.CompilerParams(
            collective_id=0, has_side_effects=True, vmem_limit_bytes=48 << 20
        ),
        name="front",
    )(
        seg_start,
        src_chan[:, None],
        strain,
        band_table(strain.shape[1], WIDTH, 0),
        back,
        place,
        high,
        low,
        phase_cos,
        phase_sin,
        smooth_mask(),
    )


def correlate_kernel(src_ref, recv_ref, basis_ref, out_ref, merged):
    groups = recv_ref.shape[0]
    rows = groups * 8
    for number in range(8):
        for low in range(0, groups, 2):
            reals, imags = [], []
            for group in (low, low + 1):
                total_re = jnp.zeros((8, NBIN), jnp.float32)
                total_im = jnp.zeros((8, NBIN), jnp.float32)
                for seg in range(NSEG):
                    a = src_ref[0, seg, number : number + 1, :].astype(jnp.float32)
                    a_re = a[:, :NBIN]
                    a_im = a[:, NBIN:]
                    b = recv_ref[group, seg].astype(jnp.float32)
                    b_re = b[:, :NBIN]
                    b_im = b[:, NBIN:]
                    total_re += a_re * b_re + a_im * b_im
                    total_im += a_re * b_im - a_im * b_re
                reals.append(total_re * (1.0 / NSEG))
                imags.append(total_im * (1.0 / NSEG))
            spot = number * rows + low * 8
            merged[spot : spot + 16, :NBIN] = jnp.concatenate(reals, axis=0).astype(jnp.bfloat16)
            merged[spot : spot + 16, NBIN:] = jnp.concatenate(imags, axis=0).astype(jnp.bfloat16)
    lagged = jnp.dot(merged[...], basis_ref[...], preferred_element_type=jnp.float32)
    out_ref[...] = lagged.astype(jnp.bfloat16)


def correlate(sources, receivers):
    tiles = sources.shape[0]
    rows = receivers.shape[0] * 8
    return pl.pallas_call(
        correlate_kernel,
        grid=(tiles,),
        in_specs=[
            pl.BlockSpec((1,) + sources.shape[1:], lambda i: (i, 0, 0, 0)),
            pl.BlockSpec(receivers.shape, lambda i: (0, 0, 0, 0)),
            pl.BlockSpec((2 * NBIN, NLAG), lambda i: (0, 0)),
        ],
        out_specs=pl.BlockSpec((8 * rows, NLAG), lambda i: (i, 0)),
        out_shape=jax.ShapeDtypeStruct((tiles * 8 * rows, NLAG), jnp.bfloat16),
        scratch_shapes=[pltpu.VMEM((8 * rows, 2 * NBIN), jnp.bfloat16)],
        name="correlate",
    )(sources, receivers, lag_table())


def on_device(strain, seg_start, src_chan):
    chan_count = lax.axis_size("chan")
    group_count = lax.axis_size("src")
    receivers, sources = front(strain, seg_start, src_chan, chan_count, group_count)
    lagged = correlate(sources, receivers)
    return lagged.reshape(-1, group_count, 8, NLAG)


def solution(mesh):
    return jax.shard_map(
        on_device,
        mesh=mesh,
        in_specs=(P("src", "chan"), P(), P()),
        out_specs=P("src", None, "chan", None),
        check_vma=False,
    )
```

```python
import functools
import math

import jax
import jax.numpy as jnp
import numpy as np
from jax import lax
from jax.experimental import pallas as pl
from jax.experimental.pallas import tpu as pltpu
from jax.sharding import PartitionSpec as P

DEC = 4
SEG = 7680
NSEG = 3
BIN_LOW = 61
NBIN = 384
NLAG = 512
TAPS = 16
PERIOD = 30
WIDTH = 256

MESH = pl.DeviceIdType.MESH


def taps():
    offsets = np.arange(TAPS)
    centred = (offsets - (TAPS - 1) / 2.0) / DEC
    coeffs = (
        np.sin(np.pi * centred)
        / (np.pi * centred)
        * (0.54 - 0.46 * np.cos(2.0 * np.pi * (offsets + 0.5) / TAPS))
    )
    return coeffs / coeffs.sum()


def band_table(samples, outputs, shift):
    coeffs = taps()
    tap = np.arange(samples)[:, None] + shift - DEC * np.arange(outputs)[None, :]
    inside = (tap >= 0) & (tap < TAPS)
    values = np.where(inside, coeffs[np.clip(tap, 0, TAPS - 1)], 0.0)
    return jnp.asarray(values, jnp.float32).astype(jnp.bfloat16)


def lag_table():
    bin_ids = BIN_LOW + np.arange(NBIN)
    delays = np.arange(NLAG) - NLAG // 2
    angles = 2.0 * np.pi * np.mod(np.outer(bin_ids, delays), SEG) / SEG
    basis = np.concatenate([np.cos(angles), -np.sin(angles)], axis=0) / np.sqrt(NBIN)
    return jnp.asarray(basis, jnp.float32).astype(jnp.bfloat16)


def inner_tables(width):
    bin_ids = BIN_LOW + np.arange(NBIN)
    inner = 2.0 * np.pi * np.mod(np.outer(np.arange(width), bin_ids), SEG) / SEG
    table = jnp.asarray(np.concatenate([np.cos(inner), -np.sin(inner)], axis=1), jnp.float32)
    high = table.astype(jnp.bfloat16)
    low = (table - high.astype(jnp.float32)).astype(jnp.bfloat16)
    return high, low


def outer_tables(width, count):
    bin_ids = BIN_LOW + np.arange(NBIN)
    outer = 2.0 * np.pi * np.mod(np.outer(width * np.arange(count), bin_ids), SEG) / SEG
    return jnp.asarray(np.cos(outer), jnp.float32), jnp.asarray(np.sin(outer), jnp.float32)


def smooth_mask():
    offsets = np.arange(NBIN)
    near = np.abs(offsets[:, None] - offsets[None, :]) <= 32
    return jnp.asarray(near.astype(np.float32)).astype(jnp.bfloat16)


def halo_tables():
    carried = TAPS - DEC
    outs = carried // DEC
    coeffs = taps()
    tap = np.arange(128)[None, :] + carried - DEC * np.arange(16)[:, None]
    inside = (tap >= 0) & (tap < TAPS) & (np.arange(16)[:, None] < outs)
    back = np.where(inside, coeffs[np.clip(tap, 0, TAPS - 1)], 0.0)
    place = np.zeros((16, 128))
    place[np.arange(outs), 128 - outs + np.arange(outs)] = 1.0
    return (
        jnp.asarray(back, jnp.float32).astype(jnp.bfloat16),
        jnp.asarray(place, jnp.float32).astype(jnp.bfloat16),
    )


def local_series(series):
    half = [
        series[:, part].astype(jnp.float32).reshape(-1, 128) for part in range(WIDTH // 128)
    ]
    return jnp.concatenate(half, axis=1)


def spectra_of(series, seg_ref, high_ref, low_ref, cos_ref, sin_ref, mask_ref, result):
    count = series.shape[0] - 1
    lane = lax.broadcasted_iota(jnp.int32, (8, WIDTH), 1)
    firsts = []
    edges = []
    for number in range(NSEG):
        start = seg_ref[number]
        first = lax.shift_right_logical(start, 8)
        offset = lax.bitwise_and(start, 255)
        opening = local_series(series[pl.ds(first, 1)])
        closing = local_series(series[pl.ds(first + PERIOD, 1)])
        edges.append(jnp.where(lane >= offset, opening, closing))
        firsts.append(first)
    flat = jnp.concatenate([local_series(series[0:count])] + edges, axis=0).astype(jnp.bfloat16)
    part = jnp.dot(flat, high_ref[...], preferred_element_type=jnp.float32)
    part = part + jnp.dot(flat, low_ref[...], preferred_element_type=jnp.float32)

    def turned(base, block):
        part_re = part[base : base + 8, :NBIN]
        part_im = part[base : base + 8, NBIN:]
        phase_cos = cos_ref[pl.ds(block, 1), :]
        phase_sin = sin_ref[pl.ds(block, 1), :]
        real = part_re * phase_cos + part_im * phase_sin
        imag = part_im * phase_cos - part_re * phase_sin
        return jnp.concatenate([real, imag], axis=1)

    for block in range(count):
        result[block] = turned(block * 8, block % PERIOD)
    scale = 1.0 / math.sqrt(SEG)
    totals = []
    for number in range(NSEG):
        first = firsts[number]
        total = turned((count + number) * 8, lax.rem(first, PERIOD))
        for block in range(1, PERIOD):
            total += result[first + block]
        totals.append(total * scale)
    total = jnp.concatenate(totals, axis=0)
    real_part = total[:, :NBIN]
    imag_part = total[:, NBIN:]
    energy = real_part * real_part + imag_part * imag_part
    smooth = jnp.zeros((NSEG * 8, NBIN), jnp.float32)
    for _ in range(2):
        piece = energy.astype(jnp.bfloat16)
        smooth += jnp.dot(piece, mask_ref[...], preferred_element_type=jnp.float32)
        energy = energy - piece.astype(jnp.float32)
    inverse = lax.rsqrt(smooth / 65.0 + 1e-05)
    white = jnp.concatenate([real_part * inverse, imag_part * inverse], axis=1)
    return white.reshape(NSEG, 8, 2 * NBIN).astype(jnp.bfloat16)


def front_kernel(
    chan_count,
    group_count,
    strain_hbm,
    back_hbm,
    band_hbm,
    src_hbm,
    place_hbm,
    high_hbm,
    low_hbm,
    cos_hbm,
    sin_hbm,
    mask_hbm,
    seg_hbm,
    basis_hbm,
    recv_out,
    src_out,
    basis,
    strain,
    back,
    band,
    src_ref,
    place,
    high,
    low,
    cos_ref,
    sin_ref,
    mask,
    seg_ref,
    dec,
    series,
    halo_send,
    halo_recv,
    picks,
    picked,
    tiles,
    src_series,
    white,
    gathered,
    src_white,
    src_gathered,
    result,
    load,
    send,
    recv,
    send_src_sem,
):
    me = lax.axis_index("chan")
    plane = lax.axis_index("src")
    rows = strain.shape[0]
    half = WIDTH // 2

    loads = [
        pltpu.make_async_copy(source, target, load.at[number])
        for number, (source, target) in enumerate(
            (
                (strain_hbm, strain),
                (back_hbm, back),
                (band_hbm, band),
                (src_hbm, src_ref),
                (place_hbm, place),
                (high_hbm, high),
                (low_hbm, low),
                (cos_hbm, cos_ref),
                (sin_hbm, sin_ref),
                (mask_hbm, mask),
                (seg_hbm, seg_ref),
                (basis_hbm, basis),
            )
        )
    ]
    for copy in loads[:4]:
        copy.start()

    barrier = pltpu.get_barrier_semaphore()

    def greet_chan(step, carry):
        peer = lax.rem(me + step, chan_count)
        pl.semaphore_signal(barrier, inc=1, device_id={"chan": peer}, device_id_type=MESH)
        return carry

    def greet_src(step, carry):
        peer = lax.rem(plane + step, group_count)
        pl.semaphore_signal(barrier, inc=1, device_id={"src": peer}, device_id_type=MESH)
        return carry

    lax.fori_loop(1, chan_count, greet_chan, 0, unroll=7)
    lax.fori_loop(1, group_count, greet_src, 0, unroll=7)
    for copy in loads[4:]:
        copy.start()

    for copy in loads[:4]:
        copy.wait()
    halo_send[...] = lax.dot_general(
        back[...],
        strain[:, :128],
        (((1,), (1,)), ((), ())),
        preferred_element_type=jnp.float32,
    ).astype(jnp.bfloat16)
    decimated = jnp.dot(strain[...], band[...], preferred_element_type=jnp.float32)
    first_half = decimated[:, :half]
    second_half = decimated[:, half:]
    dec[:, 0] = first_half.reshape(chan_count, 8, half).astype(jnp.bfloat16)
    blank = jnp.zeros((WIDTH // 128, 8, 128), jnp.bfloat16)
    series[chan_count] = blank
    src_series[chan_count] = blank
    listed = jnp.broadcast_to(src_ref[...].astype(jnp.float32), (8, src_ref.shape[1]))
    listed = (listed.T[:, :1]).astype(jnp.int32)
    channel = lax.broadcasted_iota(jnp.int32, (src_ref.shape[1], rows), 1) + plane * rows
    selector = (listed == channel).astype(jnp.float32).astype(jnp.bfloat16)

    def pick(part, values):
        chosen = jnp.dot(
            selector, values.astype(jnp.bfloat16), preferred_element_type=jnp.float32
        )
        picks[part] = chosen.reshape(group_count, -1, half).astype(jnp.bfloat16)

    pick(0, first_half)
    for copy in loads[4:]:
        copy.wait()

    pl.semaphore_wait(barrier, chan_count - 1 + group_count - 1)

    before = lax.rem(me + chan_count - 1, chan_count)
    halo = pltpu.make_async_remote_copy(
        halo_send, halo_recv, send.at[0], recv.at[0], {"chan": before}, MESH
    )
    halo.start()

    def send_picks(part):
        def body(step, carry):
            peer = lax.rem(plane + step, group_count)
            pltpu.make_async_remote_copy(
                picks.at[part, peer],
                picked.at[part, plane],
                send.at[1 + part],
                recv.at[1 + part],
                {"src": peer},
                MESH,
            ).start()
            return carry

        lax.fori_loop(1, group_count, body, 0, unroll=7)
        picked[part, plane] = picks[part, plane]

    def send_chan(part):
        def body(step, carry):
            peer = lax.rem(me + step, chan_count)
            pltpu.make_async_remote_copy(
                dec.at[peer, part],
                series.at[me, part],
                send.at[3 + part],
                recv.at[3 + part],
                {"chan": peer},
                MESH,
            ).start()
            return carry

        lax.fori_loop(1, chan_count, body, 0, unroll=7)
        series[me, part] = dec[me, part]

    send_picks(0)
    send_chan(0)
    halo.wait()
    last = jnp.where(me == chan_count - 1, 0.0, 1.0)
    tail = halo_recv[...].astype(jnp.float32) * last
    tail = jnp.dot(
        tail.T.astype(jnp.bfloat16), place[...], preferred_element_type=jnp.float32
    )
    second_half = second_half + tail
    pick(1, second_half)
    send_picks(1)
    dec[:, 1] = second_half.reshape(chan_count, 8, half).astype(jnp.bfloat16)
    send_chan(1)

    others = pl.ds(0, group_count - 1)
    for part in range(2):
        pltpu.make_async_remote_copy(
            picks.at[part, others],
            picked.at[part, others],
            send.at[1 + part],
            recv.at[1 + part],
            {"src": plane},
            MESH,
        ).wait()
        own = picked[part, 0].astype(jnp.float32)
        for number in range(1, group_count):
            own += picked[part, number].astype(jnp.float32)
        tiles[:, part] = own.reshape(-1, 8, half).astype(jnp.bfloat16)

    is_owner = lax.rem(me, 4) == 0
    owner_count = chan_count // 4

    def send_tiles(step, carry):
        peer = lax.rem(me + 4 * step - lax.rem(me, 4) + 4, chan_count)

        @pl.when(peer != me)
        def _():
            pltpu.make_async_remote_copy(
                tiles.at[lax.div(peer, 16)],
                src_series.at[me],
                send.at[5],
                recv.at[5],
                {"chan": peer},
                MESH,
            ).start()

        return carry

    lax.fori_loop(0, owner_count, send_tiles, 0)

    everyone = pl.ds(0, chan_count - 1)
    for part in range(2):
        pltpu.make_async_remote_copy(
            dec.at[everyone, part],
            series.at[everyone, part],
            send.at[3 + part],
            recv.at[3 + part],
            {"chan": me},
            MESH,
        ).wait()
    tables = (high, low, cos_ref, sin_ref, mask, result)
    white[...] = spectra_of(series, seg_ref, *tables)

    def send_white(step, carry):
        peer = lax.rem(plane + step, group_count)
        pltpu.make_async_remote_copy(
            white, gathered.at[plane], send.at[6], recv.at[6], {"src": peer}, MESH
        ).start()
        return carry

    lax.fori_loop(1, group_count, send_white, 0, unroll=7)
    gathered[plane] = white[...]

    column = lax.div(me, 16)
    region = lax.div(lax.rem(me, 16), 4)

    @pl.when(is_owner)
    def _():
        src_series[me] = tiles[column]
        arrived = src_series.at[everyone]
        pltpu.make_async_remote_copy(
            arrived, arrived, send.at[5], recv.at[5], {"chan": me}, MESH
        ).wait_recv()
        src_white[...] = spectra_of(src_series, seg_ref, *tables)

        def send_src(step, carry):
            peer = 16 * lax.div(step, 4) + 4 * region + lax.rem(step, 4)

            @pl.when(peer != me)
            def _():
                pltpu.make_async_remote_copy(
                    src_white,
                    src_gathered.at[column],
                    send_src_sem.at[step],
                    recv.at[7],
                    {"chan": peer},
                    MESH,
                ).start()

            return carry

        lax.fori_loop(0, 16, send_src, 0)
        src_gathered[column] = src_white[...]

    pltpu.make_async_remote_copy(
        gathered.at[others], gathered.at[others], send.at[6], recv.at[6], {"src": plane}, MESH
    ).wait()
    recv_out[...] = gathered[...].astype(jnp.float32)

    def wait_src(count):
        part = src_gathered.at[pl.ds(0, count)]
        pltpu.make_async_remote_copy(
            part, part, send.at[6], recv.at[7], {"chan": me}, MESH
        ).wait_recv()

    def wait_tiles(count):
        part = src_series.at[pl.ds(0, count)]
        pltpu.make_async_remote_copy(
            part, part, send.at[5], recv.at[5], {"chan": me}, MESH
        ).wait_send()

    @pl.when(is_owner)
    def _():
        wait_src(3)

        def sent_src(step, carry):
            peer = 16 * lax.div(step, 4) + 4 * region + lax.rem(step, 4)

            @pl.when(peer != me)
            def _():
                pltpu.make_async_remote_copy(
                    src_white,
                    src_gathered.at[column],
                    send_src_sem.at[step],
                    recv.at[7],
                    {"chan": peer},
                    MESH,
                ).wait_send()

            return carry

        lax.fori_loop(0, 16, sent_src, 0)
        wait_tiles(owner_count - 1)

    @pl.when(jnp.logical_not(is_owner))
    def _():
        wait_src(4)
        wait_tiles(owner_count)

    src_out[...] = src_gathered[...].astype(jnp.float32) * (1.0 / NSEG)


def front(strain, seg_start, src_chan, chan_count, group_count):
    count = src_chan.shape[0]
    share = count // group_count
    back, place = halo_tables()
    high, low = inner_tables(WIDTH)
    phase_cos, phase_sin = outer_tables(WIDTH, PERIOD)
    vmem = pl.BlockSpec(memory_space=pltpu.VMEM)
    half = jnp.bfloat16
    parts = WIDTH // 128
    operands = (
        strain,
        back,
        band_table(strain.shape[1], WIDTH, 0),
        src_chan.reshape(1, count),
        place,
        high,
        low,
        phase_cos,
        phase_sin,
        smooth_mask(),
        seg_start,
        lag_table(),
    )
    block = (parts, 8, 128)
    spectra = (NSEG, 8, 2 * NBIN)
    return pl.pallas_call(
        functools.partial(front_kernel, chan_count, group_count),
        out_shape=(
            jax.ShapeDtypeStruct((group_count,) + spectra, jnp.float32),
            jax.ShapeDtypeStruct((share // 8,) + spectra, jnp.float32),
            jax.ShapeDtypeStruct((2 * NBIN, NLAG), half),
        ),
        in_specs=[pl.BlockSpec(memory_space=pltpu.HBM)] * len(operands),
        out_specs=(vmem, vmem, vmem),
        scratch_shapes=[pltpu.VMEM(value.shape, value.dtype) for value in operands[:-2]]
        + [
            pltpu.SMEM(seg_start.shape, seg_start.dtype),
            pltpu.VMEM((chan_count,) + block, half),
            pltpu.VMEM((chan_count + 1,) + block, half),
            pltpu.VMEM((16, strain.shape[0]), half),
            pltpu.VMEM((16, strain.shape[0]), half),
            pltpu.VMEM((parts, group_count, share, 128), half),
            pltpu.VMEM((parts, group_count, share, 128), half),
            pltpu.VMEM((share // 8,) + block, half),
            pltpu.VMEM((chan_count + 1,) + block, half),
            pltpu.VMEM(spectra, half),
            pltpu.VMEM((group_count,) + spectra, half),
            pltpu.VMEM(spectra, half),
            pltpu.VMEM((share // 8,) + spectra, half),
            pltpu.VMEM((chan_count, 8, 2 * NBIN), jnp.float32),
            pltpu.SemaphoreType.DMA((len(operands),)),
            pltpu.SemaphoreType.DMA((7,)),
            pltpu.SemaphoreType.DMA((8,)),
            pltpu.SemaphoreType.DMA((16,)),
        ],
        compiler_params=pltpu.CompilerParams(
            collective_id=0, has_side_effects=True, vmem_limit_bytes=40 << 20
        ),
        name="front",
    )(*[pltpu.with_memory_space_constraint(value, pltpu.HBM) for value in operands])


def correlate_kernel(src_ref, recv_ref, basis, out_ref, merged, lagged, sems):
    groups = recv_ref.shape[0]
    rows = groups * 8
    per_step = 4
    steps = src_ref.shape[0] * 8 // per_step

    def produce(step):
        for index in range(per_step):
            tile, number = divmod(step * per_step + index, 8)
            for low in range(0, groups, 2):
                reals, imags = [], []
                for group in (low, low + 1):
                    total_re = None
                    for seg in range(NSEG):
                        a_re = src_ref[tile, seg, number : number + 1, :NBIN]
                        a_im = src_ref[tile, seg, number : number + 1, NBIN:]
                        b_re = recv_ref[group, seg, :, :NBIN]
                        b_im = recv_ref[group, seg, :, NBIN:]
                        term_re = a_re * b_re + a_im * b_im
                        term_im = a_re * b_im - a_im * b_re
                        total_re = term_re if total_re is None else total_re + term_re
                        total_im = term_im if seg == 0 else total_im + term_im
                    reals.append(total_re)
                    imags.append(total_im)
                spot = index * rows + low * 8
                merged[step % 2, spot : spot + 16, :NBIN] = jnp.concatenate(
                    reals, axis=0
                ).astype(jnp.bfloat16)
                merged[step % 2, spot : spot + 16, NBIN:] = jnp.concatenate(
                    imags, axis=0
                ).astype(jnp.bfloat16)

    copies = []
    produce(0)
    for step in range(steps):
        values = jnp.dot(merged[step % 2], basis[...], preferred_element_type=jnp.float32)
        if step + 1 < steps:
            produce(step + 1)
        lagged[step] = values.astype(jnp.bfloat16)
        size = per_step * rows
        copy = pltpu.make_async_copy(
            lagged.at[step], out_ref.at[pl.ds(step * size, size)], sems.at[step]
        )
        copy.start()
        copies.append(copy)
    for copy in copies:
        copy.wait()


def correlate(sources, receivers, basis):
    tiles = sources.shape[0]
    rows = receivers.shape[0] * 8
    steps = tiles * 2
    vmem = pl.BlockSpec(memory_space=pltpu.VMEM)
    return pl.pallas_call(
        correlate_kernel,
        in_specs=[vmem, vmem, vmem],
        out_specs=pl.BlockSpec(memory_space=pltpu.HBM),
        out_shape=jax.ShapeDtypeStruct((tiles * 8 * rows, NLAG), jnp.bfloat16),
        scratch_shapes=[
            pltpu.VMEM((2, 4 * rows, 2 * NBIN), jnp.bfloat16),
            pltpu.VMEM((steps, 4 * rows, NLAG), jnp.bfloat16),
            pltpu.SemaphoreType.DMA((steps,)),
        ],
        compiler_params=pltpu.CompilerParams(vmem_limit_bytes=40 << 20),
        name="correlate",
    )(sources, receivers, basis)


def on_device(strain, seg_start, src_chan):
    chan_count = lax.axis_size("chan")
    group_count = lax.axis_size("src")
    receivers, sources, basis = front(strain, seg_start, src_chan, chan_count, group_count)
    lagged = correlate(sources, receivers, basis)
    return lagged.reshape(-1, group_count, 8, NLAG)


def solution(mesh):
    return jax.shard_map(
        on_device,
        mesh=mesh,
        in_specs=(P("src", "chan"), P(), P()),
        out_specs=P("src", None, "chan", None),
        check_vma=False,
    )
```

```python
import functools
import math

import jax
import jax.numpy as jnp
import numpy as np
from jax import lax
from jax.experimental import pallas as pl
from jax.experimental.pallas import tpu as pltpu
from jax.sharding import PartitionSpec as P

DEC = 4
SEG = 7680
NSEG = 3
BIN_LOW = 61
NBIN = 384
NLAG = 512
TAPS = 16
PERIOD = 30
WIDTH = 256

MESH = pl.DeviceIdType.MESH


def taps():
    offsets = np.arange(TAPS)
    centred = (offsets - (TAPS - 1) / 2.0) / DEC
    coeffs = (
        np.sin(np.pi * centred)
        / (np.pi * centred)
        * (0.54 - 0.46 * np.cos(2.0 * np.pi * (offsets + 0.5) / TAPS))
    )
    return coeffs / coeffs.sum()


def band_table(samples, outputs, shift):
    coeffs = taps()
    tap = np.arange(samples)[:, None] + shift - DEC * np.arange(outputs)[None, :]
    inside = (tap >= 0) & (tap < TAPS)
    values = np.where(inside, coeffs[np.clip(tap, 0, TAPS - 1)], 0.0)
    return jnp.asarray(values, jnp.float32).astype(jnp.bfloat16)


def lag_table():
    bin_ids = BIN_LOW + np.arange(NBIN)
    delays = np.arange(NLAG) - NLAG // 2
    angles = 2.0 * np.pi * np.mod(np.outer(bin_ids, delays), SEG) / SEG
    basis = np.concatenate([np.cos(angles), -np.sin(angles)], axis=0) / np.sqrt(NBIN)
    return jnp.asarray(basis, jnp.float32).astype(jnp.bfloat16)


def inner_tables(width):
    bin_ids = BIN_LOW + np.arange(NBIN)
    inner = 2.0 * np.pi * np.mod(np.outer(np.arange(width), bin_ids), SEG) / SEG
    table = jnp.asarray(np.concatenate([np.cos(inner), -np.sin(inner)], axis=1), jnp.float32)
    high = table.astype(jnp.bfloat16)
    low = (table - high.astype(jnp.float32)).astype(jnp.bfloat16)
    return high, low


def outer_tables(width, count):
    bin_ids = BIN_LOW + np.arange(NBIN)
    outer = 2.0 * np.pi * np.mod(np.outer(width * np.arange(count), bin_ids), SEG) / SEG
    return jnp.asarray(np.cos(outer), jnp.float32), jnp.asarray(np.sin(outer), jnp.float32)


def smooth_mask():
    offsets = np.arange(NBIN)
    near = np.abs(offsets[:, None] - offsets[None, :]) <= 32
    return jnp.asarray(near.astype(np.float32)).astype(jnp.bfloat16)


def halo_tables():
    carried = TAPS - DEC
    outs = carried // DEC
    coeffs = taps()
    tap = np.arange(128)[None, :] + carried - DEC * np.arange(16)[:, None]
    inside = (tap >= 0) & (tap < TAPS) & (np.arange(16)[:, None] < outs)
    back = np.where(inside, coeffs[np.clip(tap, 0, TAPS - 1)], 0.0)
    place = np.zeros((16, 128))
    place[np.arange(outs), 128 - outs + np.arange(outs)] = 1.0
    return (
        jnp.asarray(back, jnp.float32).astype(jnp.bfloat16),
        jnp.asarray(place, jnp.float32).astype(jnp.bfloat16),
    )


def local_series(series):
    half = [
        series[:, part].astype(jnp.float32).reshape(-1, 128) for part in range(WIDTH // 128)
    ]
    return jnp.concatenate(half, axis=1)


def spectra_of(series, seg_ref, high_ref, low_ref, cos_ref, sin_ref, mask_ref, result):
    count = series.shape[0] - 1
    lane = lax.broadcasted_iota(jnp.int32, (8, WIDTH), 1)
    firsts = []
    edges = []
    for number in range(NSEG):
        start = seg_ref[number]
        first = lax.shift_right_logical(start, 8)
        offset = lax.bitwise_and(start, 255)
        opening = local_series(series[pl.ds(first, 1)])
        closing = local_series(series[pl.ds(first + PERIOD, 1)])
        edges.append(jnp.where(lane >= offset, opening, closing))
        firsts.append(first)
    flat = jnp.concatenate([local_series(series[0:count])] + edges, axis=0).astype(jnp.bfloat16)
    part = jnp.dot(flat, high_ref[...], preferred_element_type=jnp.float32)
    part = part + jnp.dot(flat, low_ref[...], preferred_element_type=jnp.float32)

    def turned(base, block):
        part_re = part[base : base + 8, :NBIN]
        part_im = part[base : base + 8, NBIN:]
        phase_cos = cos_ref[pl.ds(block, 1), :]
        phase_sin = sin_ref[pl.ds(block, 1), :]
        real = part_re * phase_cos + part_im * phase_sin
        imag = part_im * phase_cos - part_re * phase_sin
        return jnp.concatenate([real, imag], axis=1)

    for block in range(count):
        result[block] = turned(block * 8, block % PERIOD)
    scale = 1.0 / math.sqrt(SEG)
    totals = []
    for number in range(NSEG):
        first = firsts[number]
        total = turned((count + number) * 8, lax.rem(first, PERIOD))
        for block in range(1, PERIOD):
            total += result[first + block]
        totals.append(total * scale)
    total = jnp.concatenate(totals, axis=0)
    real_part = total[:, :NBIN]
    imag_part = total[:, NBIN:]
    energy = real_part * real_part + imag_part * imag_part
    smooth = jnp.zeros((NSEG * 8, NBIN), jnp.float32)
    for _ in range(2):
        piece = energy.astype(jnp.bfloat16)
        smooth += jnp.dot(piece, mask_ref[...], preferred_element_type=jnp.float32)
        energy = energy - piece.astype(jnp.float32)
    inverse = lax.rsqrt(smooth / 65.0 + 1e-05)
    white = jnp.concatenate([real_part * inverse, imag_part * inverse], axis=1)
    return white.reshape(NSEG, 8, 2 * NBIN).astype(jnp.bfloat16)


def each_group(plane, act):
    for step in (1, 2, 3, 4, 5, 6, 7):
        act(lax.rem(plane + step, 8))


def each_in_plane(me, act):
    def body(step, carry):
        act(lax.rem(me + step, 64))
        return carry

    lax.fori_loop(1, 64, body, 0, unroll=7)


def front_kernel(
    chan_count,
    group_count,
    strain_hbm,
    back_hbm,
    band_hbm,
    src_hbm,
    place_hbm,
    high_hbm,
    low_hbm,
    cos_hbm,
    sin_hbm,
    mask_hbm,
    seg_hbm,
    basis_hbm,
    recv_out,
    src_out,
    basis,
    strain,
    back,
    band,
    src_ref,
    place,
    high,
    low,
    cos_ref,
    sin_ref,
    mask,
    seg_ref,
    dec,
    series,
    halo_send,
    halo_recv,
    early,
    early_recv,
    picks,
    picked,
    tiles,
    src_series,
    white,
    gathered,
    src_white,
    src_gathered,
    result,
    load,
    send,
    recv,
    send_src_sem,
):
    me = lax.axis_index("chan")
    plane = lax.axis_index("src")
    rows = strain.shape[0]
    half = WIDTH // 2

    loads = [
        pltpu.make_async_copy(source, target, load.at[number])
        for number, (source, target) in enumerate(
            (
                (strain_hbm, strain),
                (back_hbm, back),
                (band_hbm, band),
                (src_hbm, src_ref),
                (place_hbm, place),
                (high_hbm, high),
                (low_hbm, low),
                (cos_hbm, cos_ref),
                (sin_hbm, sin_ref),
                (mask_hbm, mask),
                (seg_hbm, seg_ref),
                (basis_hbm, basis),
            )
        )
    ]
    for copy in loads[:4]:
        copy.start()

    barrier = pltpu.get_barrier_semaphore()

    def greet_chan(peer):
        pl.semaphore_signal(barrier, inc=1, device_id={"chan": peer}, device_id_type=MESH)

    before = lax.rem(me + chan_count - 1, chan_count)
    after = lax.rem(me + 1, chan_count)

    def greet_src(peer):
        pl.semaphore_signal(barrier, inc=1, device_id={"src": peer}, device_id_type=MESH)
        pl.semaphore_signal(
            barrier, inc=1, device_id={"chan": after, "src": peer}, device_id_type=MESH
        )

    each_in_plane(me, greet_chan)
    each_group(plane, greet_src)
    for copy in loads[4:]:
        copy.start()

    for copy in loads[:4]:
        copy.wait()
    halo_send[...] = lax.dot_general(
        back[...],
        strain[:, :128],
        (((1,), (1,)), ((), ())),
        preferred_element_type=jnp.float32,
    ).astype(jnp.bfloat16)
    decimated = jnp.dot(strain[...], band[...], preferred_element_type=jnp.float32)
    first_half = decimated[:, :half]
    second_half = decimated[:, half:]
    dec[:, 0] = first_half.reshape(chan_count, 8, half).astype(jnp.bfloat16)
    blank = jnp.zeros((WIDTH // 128, 8, 128), jnp.bfloat16)
    series[chan_count] = blank
    src_series[chan_count] = blank
    listed = jnp.broadcast_to(src_ref[...].astype(jnp.float32), (8, src_ref.shape[1]))
    listed = (listed.T[:, :1]).astype(jnp.int32)
    channel = lax.broadcasted_iota(jnp.int32, (src_ref.shape[1], rows), 1) + plane * rows
    selector = (listed == channel).astype(jnp.float32).astype(jnp.bfloat16)

    chosen = jnp.dot(selector, decimated.astype(jnp.bfloat16), preferred_element_type=jnp.float32)
    for part in range(2):
        piece = chosen[:, part * half : (part + 1) * half].reshape(group_count, -1, half)
        picks[:, part] = piece.astype(jnp.bfloat16)
    chosen = lax.dot_general(
        halo_send[...],
        selector,
        (((1,), (1,)), ((), ())),
        preferred_element_type=jnp.float32,
    )
    share = src_ref.shape[1] // group_count
    for group in range(group_count):
        place_at = group * share
        piece = chosen[:, place_at // 128 * 128 : place_at // 128 * 128 + 128]
        if place_at % 128:
            piece = pltpu.roll(piece, 128 - place_at % 128, 1)
        early[group] = piece.astype(jnp.bfloat16)
    for copy in loads[4:]:
        copy.wait()

    pl.semaphore_wait(barrier, chan_count - 1 + 2 * (group_count - 1))

    def send_early(peer):
        pltpu.make_async_remote_copy(
            early.at[peer],
            early_recv.at[plane],
            send.at[1],
            recv.at[1],
            {"chan": before, "src": peer},
            MESH,
        ).start()

    halo = pltpu.make_async_remote_copy(
        halo_send, halo_recv, send.at[0], recv.at[0], {"chan": before}, MESH
    )

    def send_picks(peer):
        pltpu.make_async_remote_copy(
            picks.at[peer], picked.at[plane], send.at[2], recv.at[2], {"src": peer}, MESH
        ).start()

    def send_chan(part):
        def body(peer):
            pltpu.make_async_remote_copy(
                dec.at[peer, part],
                series.at[me, part],
                send.at[3 + part],
                recv.at[3 + part],
                {"chan": peer},
                MESH,
            ).start()

        each_in_plane(me, body)
        series[me, part] = dec[me, part]

    halo.start()
    each_group(plane, send_picks)
    each_group(plane, send_early)
    send_early(plane)
    send_chan(0)
    picked[plane] = picks[plane]
    halo.wait()
    last = jnp.where(me == chan_count - 1, 0.0, 1.0)
    tail = halo_recv[...].astype(jnp.float32) * last
    tail = jnp.dot(
        tail.T.astype(jnp.bfloat16), place[...], preferred_element_type=jnp.float32
    )
    second_half = second_half + tail
    dec[:, 1] = second_half.reshape(chan_count, 8, half).astype(jnp.bfloat16)
    send_chan(1)

    others = pl.ds(0, group_count - 1)
    pltpu.make_async_remote_copy(
        early, early_recv, send.at[1], recv.at[1], {"src": plane}, MESH
    ).wait()
    tail = early_recv[0].astype(jnp.float32)
    for number in range(1, group_count):
        tail += early_recv[number].astype(jnp.float32)
    tail = jnp.dot(
        (tail * last).T[:share].astype(jnp.bfloat16), place[...], preferred_element_type=jnp.float32
    )
    pltpu.make_async_remote_copy(
        picks.at[others], picked.at[others], send.at[2], recv.at[2], {"src": plane}, MESH
    ).wait()
    for part in range(2):
        own = picked[0, part].astype(jnp.float32)
        for number in range(1, group_count):
            own += picked[number, part].astype(jnp.float32)
        if part == 1:
            own += tail
        tiles[:, part] = own.reshape(-1, 8, half).astype(jnp.bfloat16)

    column = lax.div(me, 16)
    row = lax.div(lax.rem(me, 16), 2)
    region = lax.div(row, 2)
    is_owner = lax.rem(me, 4) == 0
    owner_count = chan_count // 4
    for step in (2, 1, 3, 0):
        for side in (2, 1, 3, 0):
            tile = lax.rem(column + side, 4)
            peer = 16 * tile + 4 * lax.rem(region + step, 4)

            def send_tile(tile=tile, peer=peer):
                pltpu.make_async_remote_copy(
                    tiles.at[tile],
                    src_series.at[me],
                    send.at[5],
                    recv.at[5],
                    {"chan": peer},
                    MESH,
                ).start()

            if step == 0 and side == 0:
                pl.when(jnp.logical_not(is_owner))(send_tile)
            else:
                send_tile()

    everyone = pl.ds(0, chan_count - 1)
    for part in range(2):
        pltpu.make_async_remote_copy(
            dec.at[everyone, part],
            series.at[everyone, part],
            send.at[3 + part],
            recv.at[3 + part],
            {"chan": me},
            MESH,
        ).wait()
    tables = (high, low, cos_ref, sin_ref, mask, result)
    white[...] = spectra_of(series, seg_ref, *tables)

    turn = 1 - 2 * lax.rem(me, 2)
    for step in (3, 5, 2, 6, 1, 7):
        distance = step if step < 4 else step - 8
        peer = lax.rem(plane + step, group_count)
        number = jnp.where(turn * 3 == distance, 8, 6) if step in (3, 5) else 6
        pltpu.make_async_remote_copy(
            white, gathered.at[plane], send.at[6], recv.at[number], {"src": peer}, MESH
        ).start()
    gathered[plane] = white[...]

    def source_copy(number):
        side, place = divmod(number, 4)
        side = (2, 1, 3, 0)[side]
        other = lax.rem(lax.rem(me, 4) + 3 - place, 4)
        peer = 16 * lax.rem(column + side, 4) + 4 * region + other
        return pltpu.make_async_remote_copy(
            src_white,
            src_gathered.at[column],
            send_src_sem.at[number],
            recv.at[7],
            {"chan": peer},
            MESH,
        )

    passed = lax.rem(plane + group_count - 3 * turn, group_count)
    onward = lax.rem(plane + group_count + turn, group_count)
    forward = pltpu.make_async_remote_copy(
        gathered.at[passed],
        gathered.at[passed],
        send.at[7],
        recv.at[6],
        {"src": onward},
        MESH,
    )

    def pass_on():
        pltpu.make_async_remote_copy(
            white, gathered.at[passed], send.at[7], recv.at[8], {"src": onward}, MESH
        ).wait_recv()
        forward.start()

    @pl.when(is_owner)
    def _():
        src_series[me] = tiles[column]
        arrived = src_series.at[everyone]
        pltpu.make_async_remote_copy(
            arrived, arrived, send.at[5], recv.at[5], {"chan": me}, MESH
        ).wait_recv()
        src_white[...] = spectra_of(src_series, seg_ref, *tables)

        for number in range(15):
            source_copy(number).start()
        pass_on()
        src_gathered[column] = src_white[...]

    @pl.when(jnp.logical_not(is_owner))
    def _():
        pass_on()

    most = gathered.at[pl.ds(0, group_count - 2)]
    pltpu.make_async_remote_copy(
        most, most, send.at[6], recv.at[6], {"src": plane}, MESH
    ).wait()
    forward.wait_send()
    recv_out[...] = gathered[...].astype(jnp.float32)

    def wait_src(count):
        part = src_gathered.at[pl.ds(0, count)]
        pltpu.make_async_remote_copy(
            part, part, send.at[6], recv.at[7], {"chan": me}, MESH
        ).wait_recv()

    def wait_tiles(count):
        part = src_series.at[pl.ds(0, count)]
        pltpu.make_async_remote_copy(
            part, part, send.at[5], recv.at[5], {"chan": me}, MESH
        ).wait_send()

    @pl.when(is_owner)
    def _():
        wait_src(3)

        for number in range(15):
            source_copy(number).wait_send()
        wait_tiles(owner_count - 1)

    @pl.when(jnp.logical_not(is_owner))
    def _():
        wait_src(4)
        wait_tiles(owner_count)

    src_out[...] = src_gathered[...].astype(jnp.float32) * (1.0 / NSEG)


def front(strain, seg_start, src_chan, chan_count, group_count):
    count = src_chan.shape[0]
    share = count // group_count
    back, place = halo_tables()
    high, low = inner_tables(WIDTH)
    phase_cos, phase_sin = outer_tables(WIDTH, PERIOD)
    vmem = pl.BlockSpec(memory_space=pltpu.VMEM)
    half = jnp.bfloat16
    parts = WIDTH // 128
    operands = (
        strain,
        back,
        band_table(strain.shape[1], WIDTH, 0),
        src_chan.reshape(1, count),
        place,
        high,
        low,
        phase_cos,
        phase_sin,
        smooth_mask(),
        seg_start,
        lag_table(),
    )
    block = (parts, 8, 128)
    spectra = (NSEG, 8, 2 * NBIN)
    return pl.pallas_call(
        functools.partial(front_kernel, chan_count, group_count),
        out_shape=(
            jax.ShapeDtypeStruct((group_count,) + spectra, jnp.float32),
            jax.ShapeDtypeStruct((share // 8,) + spectra, jnp.float32),
            jax.ShapeDtypeStruct((2 * NBIN, NLAG), half),
        ),
        in_specs=[pl.BlockSpec(memory_space=pltpu.HBM)] * len(operands),
        out_specs=(vmem, vmem, vmem),
        scratch_shapes=[pltpu.VMEM(value.shape, value.dtype) for value in operands[:-2]]
        + [
            pltpu.SMEM(seg_start.shape, seg_start.dtype),
            pltpu.VMEM((chan_count,) + block, half),
            pltpu.VMEM((chan_count + 1,) + block, half),
            pltpu.VMEM((16, strain.shape[0]), half),
            pltpu.VMEM((16, strain.shape[0]), half),
            pltpu.VMEM((group_count, 16, 128), half),
            pltpu.VMEM((group_count, 16, 128), half),
            pltpu.VMEM((group_count, parts, share, 128), half),
            pltpu.VMEM((group_count, parts, share, 128), half),
            pltpu.VMEM((share // 8,) + block, half),
            pltpu.VMEM((chan_count + 1,) + block, half),
            pltpu.VMEM(spectra, half),
            pltpu.VMEM((group_count,) + spectra, half),
            pltpu.VMEM(spectra, half),
            pltpu.VMEM((share // 8,) + spectra, half),
            pltpu.VMEM((chan_count, 8, 2 * NBIN), jnp.float32),
            pltpu.SemaphoreType.DMA((len(operands),)),
            pltpu.SemaphoreType.DMA((8,)),
            pltpu.SemaphoreType.DMA((9,)),
            pltpu.SemaphoreType.DMA((15,)),
        ],
        compiler_params=pltpu.CompilerParams(
            collective_id=0, has_side_effects=True, vmem_limit_bytes=40 << 20
        ),
        name="front",
    )(*[pltpu.with_memory_space_constraint(value, pltpu.HBM) for value in operands])


def correlate_kernel(src_ref, recv_ref, basis, out_ref, merged, lagged, sems):
    groups = recv_ref.shape[0]
    rows = groups * 8
    per_step = 4
    steps = src_ref.shape[0] * 8 // per_step

    def produce(step):
        for index in range(per_step):
            tile, number = divmod(step * per_step + index, 8)
            for low in range(0, groups, 2):
                reals, imags = [], []
                for group in (low, low + 1):
                    total_re = None
                    for seg in range(NSEG):
                        a_re = src_ref[tile, seg, number : number + 1, :NBIN]
                        a_im = src_ref[tile, seg, number : number + 1, NBIN:]
                        b_re = recv_ref[group, seg, :, :NBIN]
                        b_im = recv_ref[group, seg, :, NBIN:]
                        term_re = a_re * b_re + a_im * b_im
                        term_im = a_re * b_im - a_im * b_re
                        total_re = term_re if total_re is None else total_re + term_re
                        total_im = term_im if seg == 0 else total_im + term_im
                    reals.append(total_re)
                    imags.append(total_im)
                spot = index * rows + low * 8
                merged[step % 2, spot : spot + 16, :NBIN] = jnp.concatenate(
                    reals, axis=0
                ).astype(jnp.bfloat16)
                merged[step % 2, spot : spot + 16, NBIN:] = jnp.concatenate(
                    imags, axis=0
                ).astype(jnp.bfloat16)

    copies = []
    produce(0)
    for step in range(steps):
        values = jnp.dot(merged[step % 2], basis[...], preferred_element_type=jnp.float32)
        if step + 1 < steps:
            produce(step + 1)
        lagged[step] = values.astype(jnp.bfloat16)
        size = per_step * rows
        copy = pltpu.make_async_copy(
            lagged.at[step], out_ref.at[pl.ds(step * size, size)], sems.at[step]
        )
        copy.start()
        copies.append(copy)
    for copy in copies:
        copy.wait()


def correlate(sources, receivers, basis):
    tiles = sources.shape[0]
    rows = receivers.shape[0] * 8
    steps = tiles * 2
    vmem = pl.BlockSpec(memory_space=pltpu.VMEM)
    return pl.pallas_call(
        correlate_kernel,
        in_specs=[vmem, vmem, vmem],
        out_specs=pl.BlockSpec(memory_space=pltpu.HBM),
        out_shape=jax.ShapeDtypeStruct((tiles * 8 * rows, NLAG), jnp.bfloat16),
        scratch_shapes=[
            pltpu.VMEM((2, 4 * rows, 2 * NBIN), jnp.bfloat16),
            pltpu.VMEM((steps, 4 * rows, NLAG), jnp.bfloat16),
            pltpu.SemaphoreType.DMA((steps,)),
        ],
        compiler_params=pltpu.CompilerParams(vmem_limit_bytes=40 << 20),
        name="correlate",
    )(sources, receivers, basis)


def on_device(strain, seg_start, src_chan):
    chan_count = lax.axis_size("chan")
    group_count = lax.axis_size("src")
    receivers, sources, basis = front(strain, seg_start, src_chan, chan_count, group_count)
    lagged = correlate(sources, receivers, basis)
    return lagged.reshape(-1, group_count, 8, NLAG)


def solution(mesh):
    return jax.shard_map(
        on_device,
        mesh=mesh,
        in_specs=(P("src", "chan"), P(), P()),
        out_specs=P("src", None, "chan", None),
        check_vma=False,
    )
```

```python
import functools
import math

import jax
import jax.numpy as jnp
import numpy as np
from jax import lax
from jax.experimental import pallas as pl
from jax.experimental.pallas import tpu as pltpu
from jax.sharding import PartitionSpec as P

DEC = 4
SEG = 7680
NSEG = 3
BIN_LOW = 61
NBIN = 384
NLAG = 512
TAPS = 16
PERIOD = 30
WIDTH = 256

MESH = pl.DeviceIdType.MESH


def taps():
    offsets = np.arange(TAPS)
    centred = (offsets - (TAPS - 1) / 2.0) / DEC
    coeffs = (
        np.sin(np.pi * centred)
        / (np.pi * centred)
        * (0.54 - 0.46 * np.cos(2.0 * np.pi * (offsets + 0.5) / TAPS))
    )
    return coeffs / coeffs.sum()


def band_table(samples, outputs, shift):
    coeffs = taps()
    tap = np.arange(samples)[:, None] + shift - DEC * np.arange(outputs)[None, :]
    inside = (tap >= 0) & (tap < TAPS)
    values = np.where(inside, coeffs[np.clip(tap, 0, TAPS - 1)], 0.0)
    return jnp.asarray(values, jnp.float32).astype(jnp.bfloat16)


def lag_table():
    bin_ids = BIN_LOW + np.arange(NBIN)
    delays = np.arange(NLAG) - NLAG // 2
    angles = 2.0 * np.pi * np.mod(np.outer(bin_ids, delays), SEG) / SEG
    basis = np.concatenate([np.cos(angles), -np.sin(angles)], axis=0) / np.sqrt(NBIN)
    return jnp.asarray(basis, jnp.float32).astype(jnp.bfloat16)


def inner_tables(width):
    bin_ids = BIN_LOW + np.arange(NBIN)
    inner = 2.0 * np.pi * np.mod(np.outer(np.arange(width), bin_ids), SEG) / SEG
    table = jnp.asarray(np.concatenate([np.cos(inner), -np.sin(inner)], axis=1), jnp.float32)
    high = table.astype(jnp.bfloat16)
    low = (table - high.astype(jnp.float32)).astype(jnp.bfloat16)
    return high, low


def outer_tables(width, count):
    bin_ids = BIN_LOW + np.arange(NBIN)
    outer = 2.0 * np.pi * np.mod(np.outer(width * np.arange(count), bin_ids), SEG) / SEG
    return jnp.asarray(np.cos(outer), jnp.float32), jnp.asarray(np.sin(outer), jnp.float32)


def smooth_mask():
    offsets = np.arange(NBIN)
    near = np.abs(offsets[:, None] - offsets[None, :]) <= 32
    return jnp.asarray(near.astype(np.float32)).astype(jnp.bfloat16)


def halo_tables():
    carried = TAPS - DEC
    outs = carried // DEC
    coeffs = taps()
    tap = np.arange(128)[None, :] + carried - DEC * np.arange(16)[:, None]
    inside = (tap >= 0) & (tap < TAPS) & (np.arange(16)[:, None] < outs)
    back = np.where(inside, coeffs[np.clip(tap, 0, TAPS - 1)], 0.0)
    place = np.zeros((16, 128))
    place[np.arange(outs), 128 - outs + np.arange(outs)] = 1.0
    return (
        jnp.asarray(back, jnp.float32).astype(jnp.bfloat16),
        jnp.asarray(place, jnp.float32).astype(jnp.bfloat16),
    )


def local_series(series):
    half = [
        series[:, part].astype(jnp.float32).reshape(-1, 128) for part in range(WIDTH // 128)
    ]
    return jnp.concatenate(half, axis=1)


def spectra_of(series, seg_ref, high_ref, low_ref, cos_ref, sin_ref, mask_ref, result):
    count = series.shape[0] - 1
    lane = lax.broadcasted_iota(jnp.int32, (8, WIDTH), 1)
    firsts = []
    edges = []
    for number in range(NSEG):
        start = seg_ref[number]
        first = lax.shift_right_logical(start, 8)
        offset = lax.bitwise_and(start, 255)
        opening = local_series(series[pl.ds(first, 1)])
        closing = local_series(series[pl.ds(first + PERIOD, 1)])
        edges.append(jnp.where(lane >= offset, opening, closing))
        firsts.append(first)
    flat = jnp.concatenate([local_series(series[0:count])] + edges, axis=0).astype(jnp.bfloat16)
    part = jnp.dot(flat, high_ref[...], preferred_element_type=jnp.float32)
    part = part + jnp.dot(flat, low_ref[...], preferred_element_type=jnp.float32)

    def turned(base, block):
        part_re = part[base : base + 8, :NBIN]
        part_im = part[base : base + 8, NBIN:]
        phase_cos = cos_ref[pl.ds(block, 1), :]
        phase_sin = sin_ref[pl.ds(block, 1), :]
        real = part_re * phase_cos + part_im * phase_sin
        imag = part_im * phase_cos - part_re * phase_sin
        return jnp.concatenate([real, imag], axis=1)

    for block in range(count):
        result[block] = turned(block * 8, block % PERIOD)
    scale = 1.0 / math.sqrt(SEG)
    totals = []
    for number in range(NSEG):
        first = firsts[number]
        total = turned((count + number) * 8, lax.rem(first, PERIOD))
        for block in range(1, PERIOD):
            total += result[first + block]
        totals.append(total * scale)
    total = jnp.concatenate(totals, axis=0)
    real_part = total[:, :NBIN]
    imag_part = total[:, NBIN:]
    energy = real_part * real_part + imag_part * imag_part
    smooth = jnp.zeros((NSEG * 8, NBIN), jnp.float32)
    for _ in range(2):
        piece = energy.astype(jnp.bfloat16)
        smooth += jnp.dot(piece, mask_ref[...], preferred_element_type=jnp.float32)
        energy = energy - piece.astype(jnp.float32)
    inverse = lax.rsqrt(smooth / 65.0 + 1e-05)
    white = jnp.concatenate([real_part * inverse, imag_part * inverse], axis=1)
    return white.reshape(NSEG, 8, 2 * NBIN).astype(jnp.bfloat16)


def each_group(plane, act):
    for step in (1, 2, 3, 4, 5, 6, 7):
        act(lax.rem(plane + step, 8))


def each_in_plane(me, act):
    def body(step, carry):
        act(lax.rem(me + step, 64))
        return carry

    lax.fori_loop(1, 64, body, 0, unroll=7)


def front_kernel(
    chan_count,
    group_count,
    strain_hbm,
    back_hbm,
    band_hbm,
    src_hbm,
    place_hbm,
    high_hbm,
    low_hbm,
    cos_hbm,
    sin_hbm,
    mask_hbm,
    seg_hbm,
    basis_hbm,
    recv_out,
    src_out,
    basis,
    strain,
    back,
    band,
    src_ref,
    place,
    high,
    low,
    cos_ref,
    sin_ref,
    mask,
    seg_ref,
    dec,
    series,
    halo_send,
    halo_recv,
    early,
    early_recv,
    picks,
    picked,
    tiles,
    src_series,
    white,
    gathered,
    src_white,
    src_gathered,
    result,
    load,
    send,
    recv,
    send_src_sem,
):
    me = lax.axis_index("chan")
    plane = lax.axis_index("src")
    rows = strain.shape[0]
    half = WIDTH // 2

    loads = [
        pltpu.make_async_copy(source, target, load.at[number])
        for number, (source, target) in enumerate(
            (
                (strain_hbm, strain),
                (back_hbm, back),
                (band_hbm, band),
                (src_hbm, src_ref),
                (place_hbm, place),
                (high_hbm, high),
                (low_hbm, low),
                (cos_hbm, cos_ref),
                (sin_hbm, sin_ref),
                (mask_hbm, mask),
                (seg_hbm, seg_ref),
                (basis_hbm, basis),
            )
        )
    ]
    for copy in loads[:4]:
        copy.start()

    barrier = pltpu.get_barrier_semaphore()

    def greet_chan(peer):
        pl.semaphore_signal(barrier, inc=1, device_id={"chan": peer}, device_id_type=MESH)

    before = lax.rem(me + chan_count - 1, chan_count)
    after = lax.rem(me + 1, chan_count)

    def greet_src(peer):
        pl.semaphore_signal(barrier, inc=1, device_id={"src": peer}, device_id_type=MESH)
        pl.semaphore_signal(
            barrier, inc=1, device_id={"chan": after, "src": peer}, device_id_type=MESH
        )

    each_in_plane(me, greet_chan)
    each_group(plane, greet_src)
    for copy in loads[4:]:
        copy.start()

    for copy in loads[:4]:
        copy.wait()
    halo_send[...] = lax.dot_general(
        back[...],
        strain[:, :128],
        (((1,), (1,)), ((), ())),
        preferred_element_type=jnp.float32,
    ).astype(jnp.bfloat16)
    decimated = jnp.dot(strain[...], band[...], preferred_element_type=jnp.float32)
    first_half = decimated[:, :half]
    second_half = decimated[:, half:]
    dec[:, 0] = first_half.reshape(chan_count, 8, half).astype(jnp.bfloat16)
    blank = jnp.zeros((WIDTH // 128, 8, 128), jnp.bfloat16)
    series[chan_count] = blank
    src_series[chan_count] = blank
    listed = jnp.broadcast_to(src_ref[...].astype(jnp.float32), (8, src_ref.shape[1]))
    listed = (listed.T[:, :1]).astype(jnp.int32)
    channel = lax.broadcasted_iota(jnp.int32, (src_ref.shape[1], rows), 1) + plane * rows
    selector = (listed == channel).astype(jnp.float32).astype(jnp.bfloat16)

    chosen = jnp.dot(selector, decimated.astype(jnp.bfloat16), preferred_element_type=jnp.float32)
    for part in range(2):
        piece = chosen[:, part * half : (part + 1) * half].reshape(group_count, -1, half)
        picks[:, part] = piece.astype(jnp.bfloat16)
    chosen = lax.dot_general(
        halo_send[...],
        selector,
        (((1,), (1,)), ((), ())),
        preferred_element_type=jnp.float32,
    )
    share = src_ref.shape[1] // group_count
    for group in range(group_count):
        place_at = group * share
        piece = chosen[:, place_at // 128 * 128 : place_at // 128 * 128 + 128]
        if place_at % 128:
            piece = pltpu.roll(piece, 128 - place_at % 128, 1)
        early[group] = piece.astype(jnp.bfloat16)
    for copy in loads[4:]:
        copy.wait()

    pl.semaphore_wait(barrier, chan_count - 1 + 2 * (group_count - 1))

    def send_early(peer):
        pltpu.make_async_remote_copy(
            early.at[peer],
            early_recv.at[plane],
            send.at[1],
            recv.at[1],
            {"chan": before, "src": peer},
            MESH,
        ).start()

    halo = pltpu.make_async_remote_copy(
        halo_send, halo_recv, send.at[0], recv.at[0], {"chan": before}, MESH
    )

    def send_picks(peer):
        pltpu.make_async_remote_copy(
            picks.at[peer], picked.at[plane], send.at[2], recv.at[2], {"src": peer}, MESH
        ).start()

    def send_chan(part):
        def body(peer):
            pltpu.make_async_remote_copy(
                dec.at[peer, part],
                series.at[me, part],
                send.at[3 + part],
                recv.at[3 + part],
                {"chan": peer},
                MESH,
            ).start()

        each_in_plane(me, body)
        series[me, part] = dec[me, part]

    halo.start()
    each_group(plane, send_picks)
    each_group(plane, send_early)
    send_early(plane)
    send_chan(0)
    picked[plane] = picks[plane]
    halo.wait()
    last = jnp.where(me == chan_count - 1, 0.0, 1.0)
    tail = halo_recv[...].astype(jnp.float32) * last
    tail = jnp.dot(
        tail.T.astype(jnp.bfloat16), place[...], preferred_element_type=jnp.float32
    )
    second_half = second_half + tail
    dec[:, 1] = second_half.reshape(chan_count, 8, half).astype(jnp.bfloat16)
    send_chan(1)

    others = pl.ds(0, group_count - 1)
    pltpu.make_async_remote_copy(
        early, early_recv, send.at[1], recv.at[1], {"src": plane}, MESH
    ).wait()
    tail = early_recv[0].astype(jnp.float32)
    for number in range(1, group_count):
        tail += early_recv[number].astype(jnp.float32)
    tail = jnp.dot(
        (tail * last).T[:share].astype(jnp.bfloat16), place[...], preferred_element_type=jnp.float32
    )
    pltpu.make_async_remote_copy(
        picks.at[others], picked.at[others], send.at[2], recv.at[2], {"src": plane}, MESH
    ).wait()
    for part in range(2):
        own = picked[0, part].astype(jnp.float32)
        for number in range(1, group_count):
            own += picked[number, part].astype(jnp.float32)
        if part == 1:
            own += tail
        tiles[:, part] = own.reshape(-1, 8, half).astype(jnp.bfloat16)

    column = lax.div(me, 16)
    row = lax.div(lax.rem(me, 16), 2)
    region = lax.div(row, 2)
    is_owner = lax.rem(me, 4) == 0
    owner_count = chan_count // 4
    for step in (2, 1, 3, 0):
        for side in (2, 1, 3, 0):
            tile = lax.rem(column + side, 4)
            peer = 16 * tile + 4 * lax.rem(region + step, 4)

            def send_tile(tile=tile, peer=peer):
                pltpu.make_async_remote_copy(
                    tiles.at[tile],
                    src_series.at[me],
                    send.at[5],
                    recv.at[5],
                    {"chan": peer},
                    MESH,
                ).start()

            if step == 0 and side == 0:
                pl.when(jnp.logical_not(is_owner))(send_tile)
            else:
                send_tile()

    everyone = pl.ds(0, chan_count - 1)
    for part in range(2):
        pltpu.make_async_remote_copy(
            dec.at[everyone, part],
            series.at[everyone, part],
            send.at[3 + part],
            recv.at[3 + part],
            {"chan": me},
            MESH,
        ).wait()
    tables = (high, low, cos_ref, sin_ref, mask, result)
    white[...] = spectra_of(series, seg_ref, *tables)

    turn = 1 - 2 * lax.rem(me, 2)
    for step in (3, 5, 2, 6, 1, 7):
        distance = step if step < 4 else step - 8
        peer = lax.rem(plane + step, group_count)
        number = jnp.where(turn * 3 == distance, 8, 6) if step in (3, 5) else 6
        pltpu.make_async_remote_copy(
            white, gathered.at[plane], send.at[6], recv.at[number], {"src": peer}, MESH
        ).start()
    gathered[plane] = white[...]

    def source_copy(number):
        side, place = divmod(number, 4)
        side = (2, 1, 3, 0)[side]
        other = lax.rem(lax.rem(me, 4) + 3 - place, 4)
        peer = 16 * lax.rem(column + side, 4) + 4 * region + other
        return pltpu.make_async_remote_copy(
            src_white,
            src_gathered.at[column],
            send_src_sem.at[number],
            recv.at[7],
            {"chan": peer},
            MESH,
        )

    passed = lax.rem(plane + group_count - 3 * turn, group_count)
    onward = lax.rem(plane + group_count + turn, group_count)
    forward = pltpu.make_async_remote_copy(
        gathered.at[passed],
        gathered.at[passed],
        send.at[7],
        recv.at[6],
        {"src": onward},
        MESH,
    )

    def pass_on():
        pltpu.make_async_remote_copy(
            white, gathered.at[passed], send.at[7], recv.at[8], {"src": onward}, MESH
        ).wait_recv()
        forward.start()

    @pl.when(is_owner)
    def _():
        src_series[me] = tiles[column]
        arrived = src_series.at[everyone]
        pltpu.make_async_remote_copy(
            arrived, arrived, send.at[5], recv.at[5], {"chan": me}, MESH
        ).wait_recv()
        src_white[...] = spectra_of(src_series, seg_ref, *tables)

        for number in range(15):
            source_copy(number).start()
        pass_on()
        src_gathered[column] = src_white[...]

    @pl.when(jnp.logical_not(is_owner))
    def _():
        pass_on()

    most = gathered.at[pl.ds(0, group_count - 2)]
    pltpu.make_async_remote_copy(
        most, most, send.at[6], recv.at[6], {"src": plane}, MESH
    ).wait()
    forward.wait_send()
    for pair in range(group_count // 2):
        both = [gathered[2 * pair + side].astype(jnp.float32) for side in range(2)]
        recv_out[pair] = jnp.concatenate(both, axis=1).astype(jnp.bfloat16)

    def wait_src(count):
        part = src_gathered.at[pl.ds(0, count)]
        pltpu.make_async_remote_copy(
            part, part, send.at[6], recv.at[7], {"chan": me}, MESH
        ).wait_recv()

    def wait_tiles(count):
        part = src_series.at[pl.ds(0, count)]
        pltpu.make_async_remote_copy(
            part, part, send.at[5], recv.at[5], {"chan": me}, MESH
        ).wait_send()

    @pl.when(is_owner)
    def _():
        wait_src(3)

        for number in range(15):
            source_copy(number).wait_send()
        wait_tiles(owner_count - 1)

    @pl.when(jnp.logical_not(is_owner))
    def _():
        wait_src(4)
        wait_tiles(owner_count)

    src_out[...] = src_gathered[...].astype(jnp.float32)


def front(strain, seg_start, src_chan, chan_count, group_count):
    count = src_chan.shape[0]
    share = count // group_count
    back, place = halo_tables()
    high, low = inner_tables(WIDTH)
    phase_cos, phase_sin = outer_tables(WIDTH, PERIOD)
    vmem = pl.BlockSpec(memory_space=pltpu.VMEM)
    half = jnp.bfloat16
    parts = WIDTH // 128
    operands = (
        strain,
        back,
        band_table(strain.shape[1], WIDTH, 0),
        src_chan.reshape(1, count),
        place,
        high,
        low,
        phase_cos,
        phase_sin,
        smooth_mask(),
        seg_start,
        lag_table(),
    )
    block = (parts, 8, 128)
    spectra = (NSEG, 8, 2 * NBIN)
    return pl.pallas_call(
        functools.partial(front_kernel, chan_count, group_count),
        out_shape=(
            jax.ShapeDtypeStruct((group_count // 2, NSEG, 16, 2 * NBIN), half),
            jax.ShapeDtypeStruct((share // 8,) + spectra, jnp.float32),
            jax.ShapeDtypeStruct((2 * NBIN, NLAG), half),
        ),
        in_specs=[pl.BlockSpec(memory_space=pltpu.HBM)] * len(operands),
        out_specs=(vmem, vmem, vmem),
        scratch_shapes=[pltpu.VMEM(value.shape, value.dtype) for value in operands[:-2]]
        + [
            pltpu.SMEM(seg_start.shape, seg_start.dtype),
            pltpu.VMEM((chan_count,) + block, half),
            pltpu.VMEM((chan_count + 1,) + block, half),
            pltpu.VMEM((16, strain.shape[0]), half),
            pltpu.VMEM((16, strain.shape[0]), half),
            pltpu.VMEM((group_count, 16, 128), half),
            pltpu.VMEM((group_count, 16, 128), half),
            pltpu.VMEM((group_count, parts, share, 128), half),
            pltpu.VMEM((group_count, parts, share, 128), half),
            pltpu.VMEM((share // 8,) + block, half),
            pltpu.VMEM((chan_count + 1,) + block, half),
            pltpu.VMEM(spectra, half),
            pltpu.VMEM((group_count,) + spectra, half),
            pltpu.VMEM(spectra, half),
            pltpu.VMEM((share // 8,) + spectra, half),
            pltpu.VMEM((chan_count, 8, 2 * NBIN), jnp.float32),
            pltpu.SemaphoreType.DMA((len(operands),)),
            pltpu.SemaphoreType.DMA((8,)),
            pltpu.SemaphoreType.DMA((9,)),
            pltpu.SemaphoreType.DMA((15,)),
        ],
        compiler_params=pltpu.CompilerParams(
            collective_id=0, has_side_effects=True, vmem_limit_bytes=40 << 20
        ),
        name="front",
    )(*[pltpu.with_memory_space_constraint(value, pltpu.HBM) for value in operands])


def correlate_kernel(src_ref, recv_ref, basis, out_ref, merged, lagged, sems):
    pairs = recv_ref.shape[0]
    rows = pairs * 16
    per_step = 4
    steps = src_ref.shape[0] * 8 // per_step

    def produce(step):
        for index in range(per_step):
            tile, number = divmod(step * per_step + index, 8)
            source = [
                jnp.broadcast_to(
                    src_ref[tile, seg, number : number + 1, :], (16, 2 * NBIN)
                ).astype(jnp.bfloat16)
                for seg in range(NSEG)
            ]
            for pair in range(pairs):
                total_re = total_im = None
                for seg in range(NSEG):
                    a_re = source[seg][:, :NBIN]
                    a_im = source[seg][:, NBIN:]
                    b_re = recv_ref[pair, seg, :, :NBIN]
                    b_im = recv_ref[pair, seg, :, NBIN:]
                    term_re = a_re * b_re + a_im * b_im
                    term_im = a_re * b_im - a_im * b_re
                    total_re = term_re if seg == 0 else total_re + term_re
                    total_im = term_im if seg == 0 else total_im + term_im
                spot = index * rows + pair * 16
                merged[step % 2, spot : spot + 16, :NBIN] = total_re
                merged[step % 2, spot : spot + 16, NBIN:] = total_im

    copies = []
    produce(0)
    for step in range(steps):
        values = jnp.dot(merged[step % 2], basis[...], preferred_element_type=jnp.float32)
        if step + 1 < steps:
            produce(step + 1)
        lagged[step] = (values * (1.0 / NSEG)).astype(jnp.bfloat16)
        size = per_step * rows
        copy = pltpu.make_async_copy(
            lagged.at[step], out_ref.at[pl.ds(step * size, size)], sems.at[step]
        )
        copy.start()
        copies.append(copy)
    for copy in copies:
        copy.wait()


def correlate(sources, receivers, basis):
    tiles = sources.shape[0]
    rows = receivers.shape[0] * 16
    steps = tiles * 2
    vmem = pl.BlockSpec(memory_space=pltpu.VMEM)
    return pl.pallas_call(
        correlate_kernel,
        in_specs=[vmem, vmem, vmem],
        out_specs=pl.BlockSpec(memory_space=pltpu.HBM),
        out_shape=jax.ShapeDtypeStruct((tiles * 8 * rows, NLAG), jnp.bfloat16),
        scratch_shapes=[
            pltpu.VMEM((2, 4 * rows, 2 * NBIN), jnp.bfloat16),
            pltpu.VMEM((steps, 4 * rows, NLAG), jnp.bfloat16),
            pltpu.SemaphoreType.DMA((steps,)),
        ],
        compiler_params=pltpu.CompilerParams(vmem_limit_bytes=40 << 20),
        name="correlate",
    )(sources, receivers, basis)


def on_device(strain, seg_start, src_chan):
    chan_count = lax.axis_size("chan")
    group_count = lax.axis_size("src")
    receivers, sources, basis = front(strain, seg_start, src_chan, chan_count, group_count)
    lagged = correlate(sources, receivers, basis)
    return lagged.reshape(-1, group_count, 8, NLAG)


def solution(mesh):
    return jax.shard_map(
        on_device,
        mesh=mesh,
        in_specs=(P("src", "chan"), P(), P()),
        out_specs=P("src", None, "chan", None),
        check_vma=False,
    )
```

```python
import functools
import math

import jax
import jax.numpy as jnp
import numpy as np
from jax import lax
from jax.experimental import pallas as pl
from jax.experimental.pallas import tpu as pltpu
from jax.sharding import PartitionSpec as P

DEC = 4
SEG = 7680
NSEG = 3
BIN_LOW = 61
NBIN = 384
NLAG = 512
TAPS = 16
PERIOD = 30
WIDTH = 256

MESH = pl.DeviceIdType.MESH


def taps():
    offsets = np.arange(TAPS)
    centred = (offsets - (TAPS - 1) / 2.0) / DEC
    coeffs = (
        np.sin(np.pi * centred)
        / (np.pi * centred)
        * (0.54 - 0.46 * np.cos(2.0 * np.pi * (offsets + 0.5) / TAPS))
    )
    return coeffs / coeffs.sum()


def band_table(samples, outputs, shift):
    coeffs = taps()
    tap = np.arange(samples)[:, None] + shift - DEC * np.arange(outputs)[None, :]
    inside = (tap >= 0) & (tap < TAPS)
    values = np.where(inside, coeffs[np.clip(tap, 0, TAPS - 1)], 0.0)
    return jnp.asarray(values, jnp.float32).astype(jnp.bfloat16)


def lag_table():
    bin_ids = BIN_LOW + np.arange(NBIN)
    delays = np.arange(NLAG) - NLAG // 2
    angles = 2.0 * np.pi * np.mod(np.outer(bin_ids, delays), SEG) / SEG
    basis = np.concatenate([np.cos(angles), -np.sin(angles)], axis=0) / np.sqrt(NBIN)
    return jnp.asarray(basis, jnp.float32).astype(jnp.bfloat16)


def inner_tables(width):
    bin_ids = BIN_LOW + np.arange(NBIN)
    inner = 2.0 * np.pi * np.mod(np.outer(np.arange(width), bin_ids), SEG) / SEG
    table = jnp.asarray(np.concatenate([np.cos(inner), -np.sin(inner)], axis=1), jnp.float32)
    high = table.astype(jnp.bfloat16)
    low = (table - high.astype(jnp.float32)).astype(jnp.bfloat16)
    return high, low


def outer_tables(width, count):
    bin_ids = BIN_LOW + np.arange(NBIN)
    outer = 2.0 * np.pi * np.mod(np.outer(width * np.arange(count), bin_ids), SEG) / SEG
    return jnp.asarray(np.cos(outer), jnp.float32), jnp.asarray(np.sin(outer), jnp.float32)


def smooth_mask():
    offsets = np.arange(NBIN)
    near = np.abs(offsets[:, None] - offsets[None, :]) <= 32
    return jnp.asarray(near.astype(np.float32)).astype(jnp.bfloat16)


def halo_tables():
    carried = TAPS - DEC
    outs = carried // DEC
    coeffs = taps()
    tap = np.arange(128)[None, :] + carried - DEC * np.arange(16)[:, None]
    inside = (tap >= 0) & (tap < TAPS) & (np.arange(16)[:, None] < outs)
    back = np.where(inside, coeffs[np.clip(tap, 0, TAPS - 1)], 0.0)
    place = np.zeros((16, 128))
    place[np.arange(outs), 128 - outs + np.arange(outs)] = 1.0
    return (
        jnp.asarray(back, jnp.float32).astype(jnp.bfloat16),
        jnp.asarray(place, jnp.float32).astype(jnp.bfloat16),
    )


def local_series(series):
    half = [
        series[:, part].astype(jnp.float32).reshape(-1, 128) for part in range(WIDTH // 128)
    ]
    return jnp.concatenate(half, axis=1)


def spectra_of(series, seg_ref, table_ref, cos_ref, sin_ref, mask_ref, result):
    count = series.shape[0] - 1
    lane = lax.broadcasted_iota(jnp.int32, (8, WIDTH), 1)
    firsts = []
    edges = []
    for number in range(NSEG):
        start = seg_ref[number]
        first = lax.shift_right_logical(start, 8)
        offset = lax.bitwise_and(start, 255)
        opening = local_series(series[pl.ds(first, 1)])
        closing = local_series(series[pl.ds(first + PERIOD, 1)])
        edges.append(jnp.where(lane >= offset, opening, closing))
        firsts.append(first)
    flat = jnp.concatenate([local_series(series[0:count])] + edges, axis=0).astype(jnp.bfloat16)
    twice = jnp.concatenate([flat, flat], axis=1)
    part = jnp.dot(twice, table_ref[...], preferred_element_type=jnp.float32)

    def turned(base, block):
        part_re = part[base : base + 8, :NBIN]
        part_im = part[base : base + 8, NBIN:]
        phase_cos = cos_ref[pl.ds(block, 1), :]
        phase_sin = sin_ref[pl.ds(block, 1), :]
        real = part_re * phase_cos + part_im * phase_sin
        imag = part_im * phase_cos - part_re * phase_sin
        return jnp.concatenate([real, imag], axis=1)

    for block in range(count):
        result[block] = turned(block * 8, block % PERIOD)
    scale = 1.0 / math.sqrt(SEG)
    totals = []
    for number in range(NSEG):
        first = firsts[number]
        total = turned((count + number) * 8, lax.rem(first, PERIOD))
        for block in range(1, PERIOD):
            total += result[first + block]
        totals.append(total * scale)
    total = jnp.concatenate(totals, axis=0)
    real_part = total[:, :NBIN]
    imag_part = total[:, NBIN:]
    energy = real_part * real_part + imag_part * imag_part
    smooth = jnp.zeros((NSEG * 8, NBIN), jnp.float32)
    for _ in range(2):
        piece = energy.astype(jnp.bfloat16)
        smooth += jnp.dot(piece, mask_ref[...], preferred_element_type=jnp.float32)
        energy = energy - piece.astype(jnp.float32)
    inverse = lax.rsqrt(smooth / 65.0 + 1e-05)
    white = jnp.concatenate([real_part * inverse, imag_part * inverse], axis=1)
    return white.reshape(NSEG, 8, 2 * NBIN).astype(jnp.bfloat16)


def each_group(plane, act):
    for step in (1, 2, 3, 4, 5, 6, 7):
        act(lax.rem(plane + step, 8))


def each_in_plane(me, act):
    def body(step, carry):
        act(lax.rem(me + step, 64))
        return carry

    lax.fori_loop(1, 64, body, 0, unroll=7)


def front_kernel(
    chan_count,
    group_count,
    strain_hbm,
    back_hbm,
    band_hbm,
    src_hbm,
    place_hbm,
    table_hbm,
    cos_hbm,
    sin_hbm,
    mask_hbm,
    seg_hbm,
    basis_hbm,
    recv_out,
    src_out,
    basis,
    strain,
    back,
    band,
    src_ref,
    place,
    table,
    cos_ref,
    sin_ref,
    mask,
    seg_ref,
    dec,
    series,
    halo_send,
    halo_recv,
    early,
    early_recv,
    picks,
    picked,
    tiles,
    src_series,
    white,
    gathered,
    src_white,
    src_gathered,
    result,
    load,
    send,
    recv,
    send_src_sem,
):
    me = lax.axis_index("chan")
    plane = lax.axis_index("src")
    rows = strain.shape[0]
    half = WIDTH // 2

    loads = [
        pltpu.make_async_copy(source, target, load.at[number])
        for number, (source, target) in enumerate(
            (
                (strain_hbm, strain),
                (back_hbm, back),
                (band_hbm, band),
                (src_hbm, src_ref),
                (place_hbm, place),
                (table_hbm, table),
                (cos_hbm, cos_ref),
                (sin_hbm, sin_ref),
                (mask_hbm, mask),
                (seg_hbm, seg_ref),
                (basis_hbm, basis),
            )
        )
    ]
    for copy in loads[:4]:
        copy.start()

    barrier = pltpu.get_barrier_semaphore()

    def greet_chan(peer):
        pl.semaphore_signal(barrier, inc=1, device_id={"chan": peer}, device_id_type=MESH)

    before = lax.rem(me + chan_count - 1, chan_count)
    after = lax.rem(me + 1, chan_count)

    def greet_src(peer):
        pl.semaphore_signal(barrier, inc=1, device_id={"src": peer}, device_id_type=MESH)
        pl.semaphore_signal(
            barrier, inc=1, device_id={"chan": after, "src": peer}, device_id_type=MESH
        )

    each_in_plane(me, greet_chan)
    each_group(plane, greet_src)
    for copy in loads[4:]:
        copy.start()

    for copy in loads[:4]:
        copy.wait()
    halo_send[...] = lax.dot_general(
        back[...],
        strain[:, :128],
        (((1,), (1,)), ((), ())),
        preferred_element_type=jnp.float32,
    ).astype(jnp.bfloat16)
    decimated = jnp.dot(strain[...], band[...], preferred_element_type=jnp.float32)
    first_half = decimated[:, :half]
    second_half = decimated[:, half:]
    dec[:, 0] = first_half.reshape(chan_count, 8, half).astype(jnp.bfloat16)
    blank = jnp.zeros((WIDTH // 128, 8, 128), jnp.bfloat16)
    series[chan_count] = blank
    src_series[chan_count] = blank
    listed = jnp.broadcast_to(src_ref[...].astype(jnp.float32), (8, src_ref.shape[1]))
    listed = (listed.T[:, :1]).astype(jnp.int32)
    channel = lax.broadcasted_iota(jnp.int32, (src_ref.shape[1], rows), 1) + plane * rows
    selector = (listed == channel).astype(jnp.float32).astype(jnp.bfloat16)

    chosen = jnp.dot(selector, decimated.astype(jnp.bfloat16), preferred_element_type=jnp.float32)
    for part in range(2):
        piece = chosen[:, part * half : (part + 1) * half].reshape(group_count, -1, half)
        picks[:, part] = piece.astype(jnp.bfloat16)
    chosen = lax.dot_general(
        halo_send[...],
        selector,
        (((1,), (1,)), ((), ())),
        preferred_element_type=jnp.float32,
    )
    share = src_ref.shape[1] // group_count
    for group in range(group_count):
        place_at = group * share
        piece = chosen[:, place_at // 128 * 128 : place_at // 128 * 128 + 128]
        if place_at % 128:
            piece = pltpu.roll(piece, 128 - place_at % 128, 1)
        early[group] = piece.astype(jnp.bfloat16)
    for copy in loads[4:]:
        copy.wait()

    pl.semaphore_wait(barrier, chan_count - 1 + 2 * (group_count - 1))

    def send_early(peer):
        pltpu.make_async_remote_copy(
            early.at[peer],
            early_recv.at[plane],
            send.at[1],
            recv.at[1],
            {"chan": before, "src": peer},
            MESH,
        ).start()

    halo = pltpu.make_async_remote_copy(
        halo_send, halo_recv, send.at[0], recv.at[0], {"chan": before}, MESH
    )

    def send_picks(peer):
        pltpu.make_async_remote_copy(
            picks.at[peer], picked.at[plane], send.at[2], recv.at[2], {"src": peer}, MESH
        ).start()

    def send_chan(part):
        def body(peer):
            pltpu.make_async_remote_copy(
                dec.at[peer, part],
                series.at[me, part],
                send.at[3 + part],
                recv.at[3 + part],
                {"chan": peer},
                MESH,
            ).start()

        each_in_plane(me, body)
        series[me, part] = dec[me, part]

    halo.start()
    each_group(plane, send_picks)
    each_group(plane, send_early)
    send_early(plane)
    send_chan(0)
    picked[plane] = picks[plane]
    halo.wait()
    last = jnp.where(me == chan_count - 1, 0.0, 1.0)
    tail = halo_recv[...].astype(jnp.float32) * last
    tail = jnp.dot(
        tail.T.astype(jnp.bfloat16), place[...], preferred_element_type=jnp.float32
    )
    second_half = second_half + tail
    dec[:, 1] = second_half.reshape(chan_count, 8, half).astype(jnp.bfloat16)
    send_chan(1)

    others = pl.ds(0, group_count - 1)
    pltpu.make_async_remote_copy(
        early, early_recv, send.at[1], recv.at[1], {"src": plane}, MESH
    ).wait()
    tail = early_recv[0].astype(jnp.float32)
    for number in range(1, group_count):
        tail += early_recv[number].astype(jnp.float32)
    tail = jnp.dot(
        (tail * last).T[:share].astype(jnp.bfloat16), place[...], preferred_element_type=jnp.float32
    )
    pltpu.make_async_remote_copy(
        picks.at[others], picked.at[others], send.at[2], recv.at[2], {"src": plane}, MESH
    ).wait()
    for part in range(2):
        own = picked[0, part].astype(jnp.float32)
        for number in range(1, group_count):
            own += picked[number, part].astype(jnp.float32)
        if part == 1:
            own += tail
        tiles[:, part] = own.reshape(-1, 8, half).astype(jnp.bfloat16)

    column = lax.div(me, 16)
    row = lax.div(lax.rem(me, 16), 2)
    region = lax.div(row, 2)
    is_owner = lax.rem(me, 4) == 0
    owner_count = chan_count // 4
    for step in (2, 1, 3, 0):
        for side in (2, 1, 3, 0):
            tile = lax.rem(column + side, 4)
            peer = 16 * tile + 4 * lax.rem(region + step, 4)

            def send_tile(tile=tile, peer=peer):
                pltpu.make_async_remote_copy(
                    tiles.at[tile],
                    src_series.at[me],
                    send.at[5],
                    recv.at[5],
                    {"chan": peer},
                    MESH,
                ).start()

            if step == 0 and side == 0:
                pl.when(jnp.logical_not(is_owner))(send_tile)
            else:
                send_tile()

    everyone = pl.ds(0, chan_count - 1)
    for part in range(2):
        pltpu.make_async_remote_copy(
            dec.at[everyone, part],
            series.at[everyone, part],
            send.at[3 + part],
            recv.at[3 + part],
            {"chan": me},
            MESH,
        ).wait()
    tables = (table, cos_ref, sin_ref, mask, result)
    white[...] = spectra_of(series, seg_ref, *tables)

    turn = 1 - 2 * lax.rem(me, 2)
    for step in (1, 7, 2, 6, 3, 5):
        distance = step if step < 4 else step - 8
        peer = lax.rem(plane + step, group_count)
        number = jnp.where(turn * 3 == distance, 8, 6) if step in (3, 5) else 6
        pltpu.make_async_remote_copy(
            white, gathered.at[plane], send.at[6], recv.at[number], {"src": peer}, MESH
        ).start()
    gathered[plane] = white[...]

    def source_copy(number):
        side, place = divmod(number, 4)
        side = (2, 1, 3, 0)[side]
        other = lax.rem(lax.rem(me, 4) + 3 - place, 4)
        peer = 16 * lax.rem(column + side, 4) + 4 * region + other
        return pltpu.make_async_remote_copy(
            src_white,
            src_gathered.at[column],
            send_src_sem.at[number],
            recv.at[7],
            {"chan": peer},
            MESH,
        )

    passed = lax.rem(plane + group_count - 3 * turn, group_count)
    onward = lax.rem(plane + group_count + turn, group_count)
    forward = pltpu.make_async_remote_copy(
        gathered.at[passed],
        gathered.at[passed],
        send.at[7],
        recv.at[6],
        {"src": onward},
        MESH,
    )

    def pass_on():
        pltpu.make_async_remote_copy(
            white, gathered.at[passed], send.at[7], recv.at[8], {"src": onward}, MESH
        ).wait_recv()
        forward.start()

    @pl.when(is_owner)
    def _():
        src_series[me] = tiles[column]
        arrived = src_series.at[everyone]
        pltpu.make_async_remote_copy(
            arrived, arrived, send.at[5], recv.at[5], {"chan": me}, MESH
        ).wait_recv()
        src_white[...] = spectra_of(src_series, seg_ref, *tables)

        for number in range(15):
            source_copy(number).start()
        pass_on()
        src_gathered[column] = src_white[...]

    @pl.when(jnp.logical_not(is_owner))
    def _():
        pass_on()

    most = gathered.at[pl.ds(0, group_count - 2)]
    pltpu.make_async_remote_copy(
        most, most, send.at[6], recv.at[6], {"src": plane}, MESH
    ).wait()
    forward.wait_send()
    for pair in range(group_count // 2):
        both = [gathered[2 * pair + side].astype(jnp.float32) for side in range(2)]
        recv_out[pair] = jnp.concatenate(both, axis=1).astype(jnp.bfloat16)

    def wait_src(count):
        part = src_gathered.at[pl.ds(0, count)]
        pltpu.make_async_remote_copy(
            part, part, send.at[6], recv.at[7], {"chan": me}, MESH
        ).wait_recv()

    def wait_tiles(count):
        part = src_series.at[pl.ds(0, count)]
        pltpu.make_async_remote_copy(
            part, part, send.at[5], recv.at[5], {"chan": me}, MESH
        ).wait_send()

    @pl.when(is_owner)
    def _():
        wait_src(3)

        for number in range(15):
            source_copy(number).wait_send()
        wait_tiles(owner_count - 1)

    @pl.when(jnp.logical_not(is_owner))
    def _():
        wait_src(4)
        wait_tiles(owner_count)

    src_out[...] = src_gathered[...].astype(jnp.float32)


def front(strain, seg_start, src_chan, chan_count, group_count):
    count = src_chan.shape[0]
    share = count // group_count
    back, place = halo_tables()
    table = jnp.concatenate(inner_tables(WIDTH), axis=0)
    phase_cos, phase_sin = outer_tables(WIDTH, PERIOD)
    vmem = pl.BlockSpec(memory_space=pltpu.VMEM)
    half = jnp.bfloat16
    parts = WIDTH // 128
    operands = (
        strain,
        back,
        band_table(strain.shape[1], WIDTH, 0),
        src_chan.reshape(1, count),
        place,
        table,
        phase_cos,
        phase_sin,
        smooth_mask(),
        seg_start,
        lag_table(),
    )
    block = (parts, 8, 128)
    spectra = (NSEG, 8, 2 * NBIN)
    return pl.pallas_call(
        functools.partial(front_kernel, chan_count, group_count),
        out_shape=(
            jax.ShapeDtypeStruct((group_count // 2, NSEG, 16, 2 * NBIN), half),
            jax.ShapeDtypeStruct((share // 8,) + spectra, jnp.float32),
            jax.ShapeDtypeStruct((2 * NBIN, NLAG), half),
        ),
        in_specs=[pl.BlockSpec(memory_space=pltpu.HBM)] * len(operands),
        out_specs=(vmem, vmem, vmem),
        scratch_shapes=[pltpu.VMEM(value.shape, value.dtype) for value in operands[:-2]]
        + [
            pltpu.SMEM(seg_start.shape, seg_start.dtype),
            pltpu.VMEM((chan_count,) + block, half),
            pltpu.VMEM((chan_count + 1,) + block, half),
            pltpu.VMEM((16, strain.shape[0]), half),
            pltpu.VMEM((16, strain.shape[0]), half),
            pltpu.VMEM((group_count, 16, 128), half),
            pltpu.VMEM((group_count, 16, 128), half),
            pltpu.VMEM((group_count, parts, share, 128), half),
            pltpu.VMEM((group_count, parts, share, 128), half),
            pltpu.VMEM((share // 8,) + block, half),
            pltpu.VMEM((chan_count + 1,) + block, half),
            pltpu.VMEM(spectra, half),
            pltpu.VMEM((group_count,) + spectra, half),
            pltpu.VMEM(spectra, half),
            pltpu.VMEM((share // 8,) + spectra, half),
            pltpu.VMEM((chan_count, 8, 2 * NBIN), jnp.float32),
            pltpu.SemaphoreType.DMA((len(operands),)),
            pltpu.SemaphoreType.DMA((8,)),
            pltpu.SemaphoreType.DMA((9,)),
            pltpu.SemaphoreType.DMA((15,)),
        ],
        compiler_params=pltpu.CompilerParams(
            collective_id=0, has_side_effects=True, vmem_limit_bytes=40 << 20
        ),
        name="front",
    )(*[pltpu.with_memory_space_constraint(value, pltpu.HBM) for value in operands])


def correlate_kernel(src_ref, recv_ref, basis, out_ref, merged, lagged, sems):
    pairs = recv_ref.shape[0]
    rows = pairs * 16
    per_step = 4
    steps = src_ref.shape[0] * 8 // per_step

    def produce(step):
        for index in range(per_step):
            tile, number = divmod(step * per_step + index, 8)
            source = [
                jnp.broadcast_to(
                    src_ref[tile, seg, number : number + 1, :], (16, 2 * NBIN)
                ).astype(jnp.bfloat16)
                for seg in range(NSEG)
            ]
            for pair in range(pairs):
                total_re = total_im = None
                for seg in range(NSEG):
                    a_re = source[seg][:, :NBIN]
                    a_im = source[seg][:, NBIN:]
                    b_re = recv_ref[pair, seg, :, :NBIN]
                    b_im = recv_ref[pair, seg, :, NBIN:]
                    term_re = a_re * b_re + a_im * b_im
                    term_im = a_re * b_im - a_im * b_re
                    total_re = term_re if seg == 0 else total_re + term_re
                    total_im = term_im if seg == 0 else total_im + term_im
                spot = index * rows + pair * 16
                merged[step % 2, spot : spot + 16, :NBIN] = total_re
                merged[step % 2, spot : spot + 16, NBIN:] = total_im

    copies = []
    produce(0)
    for step in range(steps):
        values = jnp.dot(merged[step % 2], basis[...], preferred_element_type=jnp.float32)
        if step + 1 < steps:
            produce(step + 1)
        lagged[step] = (values * (1.0 / NSEG)).astype(jnp.bfloat16)
        size = per_step * rows
        copy = pltpu.make_async_copy(
            lagged.at[step], out_ref.at[pl.ds(step * size, size)], sems.at[step]
        )
        copy.start()
        copies.append(copy)
    for copy in copies:
        copy.wait()


def correlate(sources, receivers, basis):
    tiles = sources.shape[0]
    rows = receivers.shape[0] * 16
    steps = tiles * 2
    vmem = pl.BlockSpec(memory_space=pltpu.VMEM)
    return pl.pallas_call(
        correlate_kernel,
        in_specs=[vmem, vmem, vmem],
        out_specs=pl.BlockSpec(memory_space=pltpu.HBM),
        out_shape=jax.ShapeDtypeStruct((tiles * 8 * rows, NLAG), jnp.bfloat16),
        scratch_shapes=[
            pltpu.VMEM((2, 4 * rows, 2 * NBIN), jnp.bfloat16),
            pltpu.VMEM((steps, 4 * rows, NLAG), jnp.bfloat16),
            pltpu.SemaphoreType.DMA((steps,)),
        ],
        compiler_params=pltpu.CompilerParams(vmem_limit_bytes=40 << 20),
        name="correlate",
    )(sources, receivers, basis)


def on_device(strain, seg_start, src_chan):
    chan_count = lax.axis_size("chan")
    group_count = lax.axis_size("src")
    receivers, sources, basis = front(strain, seg_start, src_chan, chan_count, group_count)
    lagged = correlate(sources, receivers, basis)
    return lagged.reshape(-1, group_count, 8, NLAG)


def solution(mesh):
    return jax.shard_map(
        on_device,
        mesh=mesh,
        in_specs=(P("src", "chan"), P(), P()),
        out_specs=P("src", None, "chan", None),
        check_vma=False,
    )
```

```python
import functools
import math

import jax
import jax.numpy as jnp
import numpy as np
from jax import lax
from jax.experimental import pallas as pl
from jax.experimental.pallas import tpu as pltpu
from jax.sharding import PartitionSpec as P

DEC = 4
SEG = 7680
NSEG = 3
BIN_LOW = 61
NBIN = 384
NLAG = 512
TAPS = 16
PERIOD = 30
WIDTH = 256

MESH = pl.DeviceIdType.MESH


def taps():
    offsets = np.arange(TAPS)
    centred = (offsets - (TAPS - 1) / 2.0) / DEC
    coeffs = (
        np.sin(np.pi * centred)
        / (np.pi * centred)
        * (0.54 - 0.46 * np.cos(2.0 * np.pi * (offsets + 0.5) / TAPS))
    )
    return coeffs / coeffs.sum()


def band_table(samples, outputs, shift):
    coeffs = taps()
    tap = np.arange(samples)[:, None] + shift - DEC * np.arange(outputs)[None, :]
    inside = (tap >= 0) & (tap < TAPS)
    values = np.where(inside, coeffs[np.clip(tap, 0, TAPS - 1)], 0.0)
    return jnp.asarray(values, jnp.float32).astype(jnp.bfloat16)


def lag_table():
    bin_ids = BIN_LOW + np.arange(NBIN)
    delays = np.arange(NLAG) - NLAG // 2
    angles = 2.0 * np.pi * np.mod(np.outer(bin_ids, delays), SEG) / SEG
    basis = np.concatenate([np.cos(angles), -np.sin(angles)], axis=0) / np.sqrt(NBIN)
    return jnp.asarray(basis, jnp.float32).astype(jnp.bfloat16)


def inner_tables(width):
    bin_ids = BIN_LOW + np.arange(NBIN)
    inner = 2.0 * np.pi * np.mod(np.outer(np.arange(width), bin_ids), SEG) / SEG
    table = jnp.asarray(np.concatenate([np.cos(inner), -np.sin(inner)], axis=1), jnp.float32)
    high = table.astype(jnp.bfloat16)
    low = (table - high.astype(jnp.float32)).astype(jnp.bfloat16)
    return high, low


def outer_tables(width, count):
    bin_ids = BIN_LOW + np.arange(NBIN)
    outer = 2.0 * np.pi * np.mod(np.outer(width * np.arange(count), bin_ids), SEG) / SEG
    return jnp.asarray(np.cos(outer), jnp.float32), jnp.asarray(np.sin(outer), jnp.float32)


def smooth_mask():
    offsets = np.arange(NBIN)
    near = np.abs(offsets[:, None] - offsets[None, :]) <= 32
    return jnp.asarray(near.astype(np.float32)).astype(jnp.bfloat16)


def halo_tables():
    carried = TAPS - DEC
    outs = carried // DEC
    coeffs = taps()
    tap = np.arange(128)[None, :] + carried - DEC * np.arange(16)[:, None]
    inside = (tap >= 0) & (tap < TAPS) & (np.arange(16)[:, None] < outs)
    back = np.where(inside, coeffs[np.clip(tap, 0, TAPS - 1)], 0.0)
    place = np.zeros((16, 128))
    place[np.arange(outs), 128 - outs + np.arange(outs)] = 1.0
    return (
        jnp.asarray(back, jnp.float32).astype(jnp.bfloat16),
        jnp.asarray(place, jnp.float32).astype(jnp.bfloat16),
    )


def local_series(series):
    half = [
        series[:, part].astype(jnp.float32).reshape(-1, 128) for part in range(WIDTH // 128)
    ]
    return jnp.concatenate(half, axis=1)


def spectra_of(series, seg_ref, table_ref, cos_ref, sin_ref, mask_ref, result):
    count = series.shape[0] - 1
    lane = lax.broadcasted_iota(jnp.int32, (8, WIDTH), 1)
    firsts = []
    edges = []
    for number in range(NSEG):
        start = seg_ref[number]
        first = lax.shift_right_logical(start, 8)
        offset = lax.bitwise_and(start, 255)
        opening = local_series(series[pl.ds(first, 1)])
        closing = local_series(series[pl.ds(first + PERIOD, 1)])
        edges.append(jnp.where(lane >= offset, opening, closing))
        firsts.append(first)
    flat = jnp.concatenate([local_series(series[0:count])] + edges, axis=0).astype(jnp.bfloat16)
    twice = jnp.concatenate([flat, flat], axis=1)
    part = jnp.dot(twice, table_ref[...], preferred_element_type=jnp.float32)

    def turned(base, block):
        part_re = part[base : base + 8, :NBIN]
        part_im = part[base : base + 8, NBIN:]
        phase_cos = cos_ref[pl.ds(block, 1), :]
        phase_sin = sin_ref[pl.ds(block, 1), :]
        real = part_re * phase_cos + part_im * phase_sin
        imag = part_im * phase_cos - part_re * phase_sin
        return jnp.concatenate([real, imag], axis=1)

    for block in range(count):
        result[block] = turned(block * 8, block % PERIOD)
    scale = 1.0 / math.sqrt(SEG)
    totals = []
    for number in range(NSEG):
        first = firsts[number]
        total = turned((count + number) * 8, lax.rem(first, PERIOD))
        for block in range(1, PERIOD):
            total += result[first + block]
        totals.append(total * scale)
    total = jnp.concatenate(totals, axis=0)
    real_part = total[:, :NBIN]
    imag_part = total[:, NBIN:]
    energy = real_part * real_part + imag_part * imag_part
    smooth = jnp.zeros((NSEG * 8, NBIN), jnp.float32)
    for _ in range(2):
        piece = energy.astype(jnp.bfloat16)
        smooth += jnp.dot(piece, mask_ref[...], preferred_element_type=jnp.float32)
        energy = energy - piece.astype(jnp.float32)
    inverse = lax.rsqrt(smooth / 65.0 + 1e-05)
    white = jnp.concatenate([real_part * inverse, imag_part * inverse], axis=1)
    return white.reshape(NSEG, 8, 2 * NBIN).astype(jnp.bfloat16)


def each_group(plane, act):
    for step in (1, 2, 3, 4, 5, 6, 7):
        act(lax.rem(plane + step, 8))


def each_in_plane(me, act):
    def body(step, carry):
        act(lax.rem(me + step, 64))
        return carry

    lax.fori_loop(1, 64, body, 0, unroll=7)


def front_kernel(
    chan_count,
    group_count,
    strain_hbm,
    back_hbm,
    band_hbm,
    src_hbm,
    place_hbm,
    table_hbm,
    cos_hbm,
    sin_hbm,
    mask_hbm,
    seg_hbm,
    basis_hbm,
    recv_out,
    src_out,
    basis,
    strain,
    back,
    band,
    src_ref,
    place,
    table,
    cos_ref,
    sin_ref,
    mask,
    seg_ref,
    dec,
    series,
    halo_send,
    halo_recv,
    early,
    early_recv,
    picks,
    picked,
    tiles,
    src_series,
    white,
    gathered,
    src_white,
    src_gathered,
    result,
    load,
    send,
    recv,
    send_src_sem,
):
    me = lax.axis_index("chan")
    plane = lax.axis_index("src")
    rows = strain.shape[0]
    half = WIDTH // 2

    loads = [
        pltpu.make_async_copy(source, target, load.at[number])
        for number, (source, target) in enumerate(
            (
                (strain_hbm, strain),
                (back_hbm, back),
                (band_hbm, band),
                (src_hbm, src_ref),
                (place_hbm, place),
                (table_hbm, table),
                (cos_hbm, cos_ref),
                (sin_hbm, sin_ref),
                (mask_hbm, mask),
                (seg_hbm, seg_ref),
                (basis_hbm, basis),
            )
        )
    ]
    for copy in loads[:4]:
        copy.start()

    barrier = pltpu.get_barrier_semaphore()

    def greet_chan(peer):
        pl.semaphore_signal(barrier, inc=1, device_id={"chan": peer}, device_id_type=MESH)

    before = lax.rem(me + chan_count - 1, chan_count)
    after = lax.rem(me + 1, chan_count)

    def greet_src(peer):
        pl.semaphore_signal(barrier, inc=1, device_id={"src": peer}, device_id_type=MESH)
        pl.semaphore_signal(
            barrier, inc=1, device_id={"chan": after, "src": peer}, device_id_type=MESH
        )

    each_in_plane(me, greet_chan)
    each_group(plane, greet_src)
    for copy in loads[4:]:
        copy.start()

    for copy in loads[:4]:
        copy.wait()
    halo_send[...] = lax.dot_general(
        back[...],
        strain[:, :128],
        (((1,), (1,)), ((), ())),
        preferred_element_type=jnp.float32,
    ).astype(jnp.bfloat16)
    decimated = jnp.dot(strain[...], band[...], preferred_element_type=jnp.float32)
    first_half = decimated[:, :half]
    second_half = decimated[:, half:]
    dec[:, 0] = first_half.reshape(chan_count, 8, half).astype(jnp.bfloat16)
    blank = jnp.zeros((WIDTH // 128, 8, 128), jnp.bfloat16)
    series[chan_count] = blank
    src_series[chan_count] = blank
    listed = jnp.broadcast_to(src_ref[...].astype(jnp.float32), (8, src_ref.shape[1]))
    listed = (listed.T[:, :1]).astype(jnp.int32)
    channel = lax.broadcasted_iota(jnp.int32, (src_ref.shape[1], rows), 1) + plane * rows
    selector = (listed == channel).astype(jnp.float32).astype(jnp.bfloat16)

    chosen = jnp.dot(selector, decimated.astype(jnp.bfloat16), preferred_element_type=jnp.float32)
    for part in range(2):
        piece = chosen[:, part * half : (part + 1) * half].reshape(group_count, -1, half)
        picks[:, part] = piece.astype(jnp.bfloat16)
    chosen = lax.dot_general(
        halo_send[...],
        selector,
        (((1,), (1,)), ((), ())),
        preferred_element_type=jnp.float32,
    )
    share = src_ref.shape[1] // group_count
    for group in range(group_count):
        place_at = group * share
        piece = chosen[:, place_at // 128 * 128 : place_at // 128 * 128 + 128]
        if place_at % 128:
            piece = pltpu.roll(piece, 128 - place_at % 128, 1)
        early[group] = piece.astype(jnp.bfloat16)
    for copy in loads[4:]:
        copy.wait()

    pl.semaphore_wait(barrier, chan_count - 1 + 2 * (group_count - 1))

    def send_early(peer):
        pltpu.make_async_remote_copy(
            early.at[peer],
            early_recv.at[plane],
            send.at[1],
            recv.at[1],
            {"chan": before, "src": peer},
            MESH,
        ).start()

    halo = pltpu.make_async_remote_copy(
        halo_send, halo_recv, send.at[0], recv.at[0], {"chan": before}, MESH
    )

    def send_picks(peer):
        pltpu.make_async_remote_copy(
            picks.at[peer], picked.at[plane], send.at[2], recv.at[2], {"src": peer}, MESH
        ).start()

    def send_chan(part):
        def body(peer):
            pltpu.make_async_remote_copy(
                dec.at[peer, part],
                series.at[me, part],
                send.at[3 + part],
                recv.at[3 + part],
                {"chan": peer},
                MESH,
            ).start()

        each_in_plane(me, body)
        series[me, part] = dec[me, part]

    halo.start()
    each_group(plane, send_picks)
    each_group(plane, send_early)
    send_early(plane)
    send_chan(0)
    picked[plane] = picks[plane]
    halo.wait()
    last = jnp.where(me == chan_count - 1, 0.0, 1.0)
    tail = halo_recv[...].astype(jnp.float32) * last
    tail = jnp.dot(
        tail.T.astype(jnp.bfloat16), place[...], preferred_element_type=jnp.float32
    )
    second_half = second_half + tail
    dec[:, 1] = second_half.reshape(chan_count, 8, half).astype(jnp.bfloat16)
    send_chan(1)

    others = pl.ds(0, group_count - 1)
    pltpu.make_async_remote_copy(
        early, early_recv, send.at[1], recv.at[1], {"src": plane}, MESH
    ).wait()
    tail = early_recv[0].astype(jnp.float32)
    for number in range(1, group_count):
        tail += early_recv[number].astype(jnp.float32)
    tail = jnp.dot(
        (tail * last).T[:share].astype(jnp.bfloat16), place[...], preferred_element_type=jnp.float32
    )
    pltpu.make_async_remote_copy(
        picks.at[others], picked.at[others], send.at[2], recv.at[2], {"src": plane}, MESH
    ).wait()
    for part in range(2):
        own = picked[0, part].astype(jnp.float32)
        for number in range(1, group_count):
            own += picked[number, part].astype(jnp.float32)
        if part == 1:
            own += tail
        tiles[:, part] = own.reshape(-1, 8, half).astype(jnp.bfloat16)

    column = lax.div(me, 16)
    row = lax.div(lax.rem(me, 16), 2)
    region = lax.div(row, 2)
    is_owner = lax.rem(me, 4) == 0
    owner_count = chan_count // 4
    for step in (2, 1, 3, 0):
        for side in (2, 1, 3, 0):
            tile = lax.rem(column + side, 4)
            peer = 16 * tile + 4 * lax.rem(region + step, 4)

            def send_tile(tile=tile, peer=peer):
                pltpu.make_async_remote_copy(
                    tiles.at[tile],
                    src_series.at[me],
                    send.at[5],
                    recv.at[5],
                    {"chan": peer},
                    MESH,
                ).start()

            if step == 0 and side == 0:
                pl.when(jnp.logical_not(is_owner))(send_tile)
            else:
                send_tile()

    everyone = pl.ds(0, chan_count - 1)
    for part in range(2):
        pltpu.make_async_remote_copy(
            dec.at[everyone, part],
            series.at[everyone, part],
            send.at[3 + part],
            recv.at[3 + part],
            {"chan": me},
            MESH,
        ).wait()
    tables = (table, cos_ref, sin_ref, mask, result)
    white[...] = spectra_of(series, seg_ref, *tables)

    turn = 1 - 2 * lax.rem(me, 2)
    for step in (3, 5, 2, 6, 1, 7):
        distance = step if step < 4 else step - 8
        peer = lax.rem(plane + step, group_count)
        number = jnp.where(turn * 3 == distance, 8, 6) if step in (3, 5) else 6
        pltpu.make_async_remote_copy(
            white, gathered.at[plane], send.at[6], recv.at[number], {"src": peer}, MESH
        ).start()
    gathered[plane] = white[...]

    def source_copy(number):
        side, place = divmod(number, 4)
        side = (2, 1, 3, 0)[side]
        other = lax.rem(lax.rem(me, 4) + 3 - place, 4)
        peer = 16 * lax.rem(column + side, 4) + 4 * region + other
        return pltpu.make_async_remote_copy(
            src_white,
            src_gathered.at[column],
            send_src_sem.at[number],
            recv.at[7],
            {"chan": peer},
            MESH,
        )

    passed = lax.rem(plane + group_count - 3 * turn, group_count)
    onward = lax.rem(plane + group_count + turn, group_count)
    forward = pltpu.make_async_remote_copy(
        gathered.at[passed],
        gathered.at[passed],
        send.at[7],
        recv.at[6],
        {"src": onward},
        MESH,
    )

    def pass_on():
        pltpu.make_async_remote_copy(
            white, gathered.at[passed], send.at[7], recv.at[8], {"src": onward}, MESH
        ).wait_recv()
        forward.start()

    @pl.when(is_owner)
    def _():
        src_series[me] = tiles[column]
        arrived = src_series.at[everyone]
        pltpu.make_async_remote_copy(
            arrived, arrived, send.at[5], recv.at[5], {"chan": me}, MESH
        ).wait_recv()
        src_white[...] = spectra_of(src_series, seg_ref, *tables)

        for number in range(15):
            source_copy(number).start()
        pass_on()
        src_gathered[column] = src_white[...]

    @pl.when(jnp.logical_not(is_owner))
    def _():
        pass_on()

    most = gathered.at[pl.ds(0, group_count - 2)]
    pltpu.make_async_remote_copy(
        most, most, send.at[6], recv.at[6], {"src": plane}, MESH
    ).wait()
    forward.wait_send()
    for pair in range(group_count // 2):
        both = [gathered[2 * pair + side].astype(jnp.float32) for side in range(2)]
        recv_out[pair] = jnp.concatenate(both, axis=1).astype(jnp.bfloat16)

    def wait_src(count):
        part = src_gathered.at[pl.ds(0, count)]
        pltpu.make_async_remote_copy(
            part, part, send.at[6], recv.at[7], {"chan": me}, MESH
        ).wait_recv()

    def wait_tiles(count):
        part = src_series.at[pl.ds(0, count)]
        pltpu.make_async_remote_copy(
            part, part, send.at[5], recv.at[5], {"chan": me}, MESH
        ).wait_send()

    @pl.when(is_owner)
    def _():
        wait_src(3)

        for number in range(15):
            source_copy(number).wait_send()
        wait_tiles(owner_count - 1)

    @pl.when(jnp.logical_not(is_owner))
    def _():
        wait_src(4)
        wait_tiles(owner_count)

    src_out[...] = src_gathered[...].astype(jnp.float32)


def front(strain, seg_start, src_chan, chan_count, group_count):
    count = src_chan.shape[0]
    share = count // group_count
    back, place = halo_tables()
    table = jnp.concatenate(inner_tables(WIDTH), axis=0)
    phase_cos, phase_sin = outer_tables(WIDTH, PERIOD)
    vmem = pl.BlockSpec(memory_space=pltpu.VMEM)
    half = jnp.bfloat16
    parts = WIDTH // 128
    operands = (
        strain,
        back,
        band_table(strain.shape[1], WIDTH, 0),
        src_chan.reshape(1, count),
        place,
        table,
        phase_cos,
        phase_sin,
        smooth_mask(),
        seg_start,
        lag_table(),
    )
    block = (parts, 8, 128)
    spectra = (NSEG, 8, 2 * NBIN)
    return pl.pallas_call(
        functools.partial(front_kernel, chan_count, group_count),
        out_shape=(
            jax.ShapeDtypeStruct((group_count // 2, NSEG, 16, 2 * NBIN), half),
            jax.ShapeDtypeStruct((share // 8,) + spectra, jnp.float32),
            jax.ShapeDtypeStruct((2 * NBIN, NLAG), half),
        ),
        in_specs=[pl.BlockSpec(memory_space=pltpu.HBM)] * len(operands),
        out_specs=(vmem, vmem, vmem),
        scratch_shapes=[pltpu.VMEM(value.shape, value.dtype) for value in operands[:-2]]
        + [
            pltpu.SMEM(seg_start.shape, seg_start.dtype),
            pltpu.VMEM((chan_count,) + block, half),
            pltpu.VMEM((chan_count + 1,) + block, half),
            pltpu.VMEM((16, strain.shape[0]), half),
            pltpu.VMEM((16, strain.shape[0]), half),
            pltpu.VMEM((group_count, 16, 128), half),
            pltpu.VMEM((group_count, 16, 128), half),
            pltpu.VMEM((group_count, parts, share, 128), half),
            pltpu.VMEM((group_count, parts, share, 128), half),
            pltpu.VMEM((share // 8,) + block, half),
            pltpu.VMEM((chan_count + 1,) + block, half),
            pltpu.VMEM(spectra, half),
            pltpu.VMEM((group_count,) + spectra, half),
            pltpu.VMEM(spectra, half),
            pltpu.VMEM((share // 8,) + spectra, half),
            pltpu.VMEM((chan_count, 8, 2 * NBIN), jnp.float32),
            pltpu.SemaphoreType.DMA((len(operands),)),
            pltpu.SemaphoreType.DMA((8,)),
            pltpu.SemaphoreType.DMA((9,)),
            pltpu.SemaphoreType.DMA((15,)),
        ],
        compiler_params=pltpu.CompilerParams(
            collective_id=0, has_side_effects=True, vmem_limit_bytes=40 << 20
        ),
        name="front",
    )(*[pltpu.with_memory_space_constraint(value, pltpu.HBM) for value in operands])


def correlate_kernel(src_ref, recv_ref, basis, out_ref, merged, lagged, sems):
    pairs = recv_ref.shape[0]
    rows = pairs * 16
    per_step = 4
    steps = src_ref.shape[0] * 8 // per_step

    def produce(step):
        for index in range(per_step):
            tile, number = divmod(step * per_step + index, 8)
            source = [
                jnp.broadcast_to(
                    src_ref[tile, seg, number : number + 1, :], (16, 2 * NBIN)
                ).astype(jnp.bfloat16)
                for seg in range(NSEG)
            ]
            for pair in range(pairs):
                total_re = total_im = None
                for seg in range(NSEG):
                    a_re = source[seg][:, :NBIN]
                    a_im = source[seg][:, NBIN:]
                    b_re = recv_ref[pair, seg, :, :NBIN]
                    b_im = recv_ref[pair, seg, :, NBIN:]
                    term_re = a_re * b_re + a_im * b_im
                    term_im = a_re * b_im - a_im * b_re
                    total_re = term_re if seg == 0 else total_re + term_re
                    total_im = term_im if seg == 0 else total_im + term_im
                spot = index * rows + pair * 16
                merged[step % 2, spot : spot + 16, :NBIN] = total_re
                merged[step % 2, spot : spot + 16, NBIN:] = total_im

    copies = []
    produce(0)
    for step in range(steps):
        values = jnp.dot(merged[step % 2], basis[...], preferred_element_type=jnp.float32)
        if step + 1 < steps:
            produce(step + 1)
        lagged[step] = (values * (1.0 / NSEG)).astype(jnp.bfloat16)
        size = per_step * rows
        copy = pltpu.make_async_copy(
            lagged.at[step], out_ref.at[pl.ds(step * size, size)], sems.at[step]
        )
        copy.start()
        copies.append(copy)
    for copy in copies:
        copy.wait()


def correlate(sources, receivers, basis):
    tiles = sources.shape[0]
    rows = receivers.shape[0] * 16
    steps = tiles * 2
    vmem = pl.BlockSpec(memory_space=pltpu.VMEM)
    return pl.pallas_call(
        correlate_kernel,
        in_specs=[vmem, vmem, vmem],
        out_specs=pl.BlockSpec(memory_space=pltpu.HBM),
        out_shape=jax.ShapeDtypeStruct((tiles * 8 * rows, NLAG), jnp.bfloat16),
        scratch_shapes=[
            pltpu.VMEM((2, 4 * rows, 2 * NBIN), jnp.bfloat16),
            pltpu.VMEM((steps, 4 * rows, NLAG), jnp.bfloat16),
            pltpu.SemaphoreType.DMA((steps,)),
        ],
        compiler_params=pltpu.CompilerParams(vmem_limit_bytes=40 << 20),
        name="correlate",
    )(sources, receivers, basis)


def on_device(strain, seg_start, src_chan):
    chan_count = lax.axis_size("chan")
    group_count = lax.axis_size("src")
    receivers, sources, basis = front(strain, seg_start, src_chan, chan_count, group_count)
    lagged = correlate(sources, receivers, basis)
    return lagged.reshape(-1, group_count, 8, NLAG)


def solution(mesh):
    return jax.shard_map(
        on_device,
        mesh=mesh,
        in_specs=(P("src", "chan"), P(), P()),
        out_specs=P("src", None, "chan", None),
        check_vma=False,
    )
```
